512 devices in a mesh: tick: 64 (over y, z_hi, core), wire: 8 (over z_lo, x).
Axes of the slice: x: 4, y: 8, z: 8 (z_hi: 4, z_lo: 2; z = z_hi * 2 + z_lo), core: 2. Of those that a mesh axis runs over, the one named last changes fastest.
Arguments:
- signal: float32 [16, 512, 8192], P(None, 'wire', 'tick'), may hold values from -6 to 6
- kernel_front: float32 [16, 3, 9], replicated, may hold values from -1.25 to 1.25
- mixing_front: float32 [16, 16], replicated, may hold values from -1.5 to 1.5
- offset_front: float32 [16], replicated, may hold values from -2 to 2
- kernel_back: float32 [16, 3, 9], replicated, may hold values from -1.25 to 1.25
- mixing_back: float32 [16, 16], replicated, may hold values from -1.5 to 1.5
- offset_back: float32 [16], replicated, may hold values from -2 to 2
- upstream: float32 [16, 512, 8192], P(None, 'wire', 'tick'), may hold values from -13 to 13
Outputs:
- response: float32 [16, 512, 8192], P(None, 'wire', 'tick')
- signal_grad: float32 [16, 512, 8192], P(None, 'wire', 'tick')
- kernel_front_grad: float32 [16, 3, 9], replicated
- mixing_front_grad: float32 [16, 16], replicated
- offset_front_grad: float32 [16], replicated
- kernel_back_grad: float32 [16, 3, 9], replicated
- mixing_back_grad: float32 [16, 16], replicated
- offset_back_grad: float32 [16], replicated
The draws below stay inside these ranges and needn't reach their ends.
All inputs are finite; a program needn't handle non-finite values.
Results may differ from the reference program's by a relative error of at most 0.0003.
Values sent between devices are 32-bit elements; how exact they have to be, the bound alone decides.
No kernel may reach another device: no remote copies, remote signals or barrier semaphores. Data moves between devices by JAX's collectives and lax.ppermute only.
A program may use at most 64 MiB of HBM per device.

```python
import math
import jax
import jax.numpy as jnp
from jax import lax

C = 16
TICK_DILATION = 8
WIRES = 512
TICKS = 8192


def draw_upstream(key, part):
    ticks_rel = jnp.arange(TICKS).astype(jnp.float32) / (TICKS - 1)
    wires_rel = jnp.arange(WIRES).astype(jnp.float32) / (WIRES - 1)
    ramp = jnp.power(3.0, wires_rel[:, None] + ticks_rel[None, :] - 1.0)
    normal = jnp.clip(jax.random.normal(key, (C, WIRES, TICKS), jnp.float32), -4.0, 4.0)
    return normal * ramp[None, :, :]


def block_scale(stream_key, extent, pieces, smallest, largest):
    factor_of = 1.0
    for position, blocks in pieces:
        steps = jax.random.uniform(jax.random.fold_in(jax.random.fold_in(stream_key, 6), position), (blocks,), jnp.float32, smallest / len(pieces), largest / len(pieces))
        factor_of = factor_of * jnp.repeat(jnp.exp(steps), extent[position] // blocks).reshape((-1,) + (1,) * (len(extent) - 1 - position))
    return factor_of


def noise(own_key, dims, width, bound, shards=(), kind=jnp.bfloat16):
    gain = block_scale(own_key, dims, shards, -0.22, 0.18) if shards else 1.0
    array = jax.random.normal(own_key, dims, jnp.float32) * width * gain
    return jnp.minimum(jnp.maximum(array, -bound), bound).astype(kind)


def setup_inputs(seed: int = 0) -> dict:
    seeds = jax.random.split(jax.random.key(seed), 9)
    return {
        "signal": noise(seeds[0], (C, WIRES, TICKS), 1.0, 6.0, ((1, 8), (2, 64)), jnp.float32),
        "kernel_front": noise(seeds[1], (C, 3, 9), 27 ** -0.5, 1.25, (), jnp.float32),
        "mixing_front": noise(seeds[2], (C, C), C ** -0.5, 1.5, (), jnp.float32),
        "offset_front": noise(seeds[3], (C,), 0.5, 2.0, (), jnp.float32),
        "kernel_back": noise(seeds[4], (C, 3, 9), 27 ** -0.5, 1.25, (), jnp.float32),
        "mixing_back": noise(seeds[5], (C, C), C ** -0.5, 1.5, (), jnp.float32),
        "offset_back": noise(seeds[6], (C,), 0.5, 2.0, (), jnp.float32),
        "upstream": draw_upstream(jax.random.fold_in(seeds[8], 71), 0),
    }


def depthwise(padded_input, kernel_weight, row_count, column_count):
    total_sum = jnp.zeros((padded_input.shape[0], row_count, column_count), jnp.float32)
    for row_index in range(3):
        for column_index in range(9):
            total_sum = total_sum + kernel_weight[:, row_index, column_index][:, None, None] * padded_input[:, row_index:row_index + row_count, TICK_DILATION * column_index:TICK_DILATION * column_index + column_count]
    return total_sum

def tap_grads(upward_gradient, padded_input):
    row_count = upward_gradient.shape[1]
    column_count = upward_gradient.shape[2]
    text_lines = []
    for row_index in range(3):
        text_lines.append(jnp.stack([lax.optimization_barrier(jnp.sum(upward_gradient * padded_input[:, row_index:row_index + row_count, TICK_DILATION * column_index:TICK_DILATION * column_index + column_count], axis=(1, 2))) for column_index in range(9)], axis=1))
    return jnp.stack(text_lines, axis=1)

def mixing(matrix, field, offset):
    return jnp.einsum('oc,cwt->owt', matrix, field, precision=lax.Precision.HIGHEST) + offset[:, None, None]

def slope(preact):
    sig = jax.nn.sigmoid(preact)
    return sig * (1.0 + preact * (1.0 - sig))

def widen(field):
    kernel_extent = 4 * TICK_DILATION
    return jnp.pad(field, ((0, 0), (1, 1), (kernel_extent, kernel_extent)))

def reference(signal, kernel_front, mixing_front, offset_front, kernel_back, mixing_back, offset_back, upstream):
    row_count = signal.shape[1]
    column_count = signal.shape[2]
    padded_in = widen(signal)
    taps_front = depthwise(padded_in, kernel_front, row_count, column_count)
    pre_front = mixing(mixing_front, taps_front, offset_front)
    act_front = jax.nn.silu(pre_front)
    padded_act = widen(act_front)
    taps_back = depthwise(padded_act, kernel_back, row_count, column_count)
    pre_back = mixing(mixing_back, taps_back, offset_back)
    response = jax.nn.silu(pre_back)
    grad_back = upstream * slope(pre_back)
    gmix_back = jnp.einsum('owt,cwt->oc', grad_back, taps_back, precision=lax.Precision.HIGHEST)
    gbias_back = lax.optimization_barrier(jnp.sum(grad_back, axis=(1, 2)))
    under_back = jnp.einsum('oc,owt->cwt', mixing_back, grad_back, precision=lax.Precision.HIGHEST)
    gkern_back = tap_grads(under_back, padded_act)
    into_front = depthwise(widen(under_back), kernel_back[:, ::-1, ::-1], row_count, column_count)
    grad_front = into_front * slope(pre_front)
    gmix_front = jnp.einsum('owt,cwt->oc', grad_front, taps_front, precision=lax.Precision.HIGHEST)
    gbias_front = lax.optimization_barrier(jnp.sum(grad_front, axis=(1, 2)))
    under_front = jnp.einsum('oc,owt->cwt', mixing_front, grad_front, precision=lax.Precision.HIGHEST)
    gkern_front = tap_grads(under_front, padded_in)
    signal_grad = depthwise(widen(under_front), kernel_front[:, ::-1, ::-1], row_count, column_count)
    factor = 1.0 / math.sqrt(row_count * column_count)
    return (response, signal_grad, gkern_front * factor, gmix_front * factor, gbias_front * factor, gkern_back * factor, gmix_back * factor, gbias_back * factor)
```

```python
import math

import jax
import jax.numpy as jnp
from jax import lax
from jax.sharding import Mesh, PartitionSpec as P

TICK_DILATION = 8
TICK = ("y", "z_hi", "core")
WIRE = ("z_lo", "x")
REDUCTION_ORDER = ("core", "x", ("z_hi", "z_lo"), "y")


def with_halo(block, sides, width):
    for axis, dim in sides:
        count = lax.axis_size(axis)
        forward = [(i, i + 1) for i in range(count - 1)]
        backward = [(target, source) for source, target in forward]
        low = lax.ppermute(
            lax.slice_in_dim(block, block.shape[dim] - width, None, axis=dim), axis, forward
        )
        high = lax.ppermute(lax.slice_in_dim(block, 0, width, axis=dim), axis, backward)
        block = jnp.concatenate([low, block, high], axis=dim)
    return block


def spread(field, tick_deep, wire_deep):
    longer = with_halo(field, ((TICK, 2),), tick_deep)
    return with_halo(longer, ((WIRE, 1),), wire_deep)


def depthwise(padded_input, kernel_weight, row_count, column_count):
    total_sum = jnp.zeros((padded_input.shape[0], row_count, column_count), jnp.float32)
    for row_index in range(3):
        for column_index in range(9):
            total_sum = (
                total_sum
                + kernel_weight[:, row_index, column_index][:, None, None]
                * padded_input[
                    :,
                    row_index : row_index + row_count,
                    TICK_DILATION * column_index : TICK_DILATION * column_index + column_count,
                ]
            )
    return total_sum


def tap_grads(upward_gradient, padded_input):
    row_count = upward_gradient.shape[1]
    column_count = upward_gradient.shape[2]
    text_lines = []
    for row_index in range(3):
        text_lines.append(
            jnp.stack(
                [
                    jnp.sum(
                        upward_gradient
                        * padded_input[
                            :,
                            row_index : row_index + row_count,
                            TICK_DILATION * column_index : TICK_DILATION * column_index
                            + column_count,
                        ],
                        axis=(1, 2),
                    )
                    for column_index in range(9)
                ],
                axis=1,
            )
        )
    return jnp.stack(text_lines, axis=1)


def mixing(matrix, field, offset):
    return (
        jnp.einsum("oc,cwt->owt", matrix, field, precision=lax.Precision.HIGHEST)
        + offset[:, None, None]
    )


def slope(preact):
    sig = jax.nn.sigmoid(preact)
    return sig * (1.0 + preact * (1.0 - sig))


def per_device(
    signal,
    kernel_front,
    mixing_front,
    offset_front,
    kernel_back,
    mixing_back,
    offset_back,
    upstream,
):
    row_count = signal.shape[1]
    column_count = signal.shape[2]
    kernel_extent = 4 * TICK_DILATION
    padded_in = spread(signal, kernel_extent, 1)
    taps_front = depthwise(padded_in, kernel_front, row_count, column_count)
    pre_front = mixing(mixing_front, taps_front, offset_front)
    padded_act = spread(jax.nn.silu(pre_front), kernel_extent, 1)
    taps_back = depthwise(padded_act, kernel_back, row_count, column_count)
    pre_back = mixing(mixing_back, taps_back, offset_back)
    response = jax.nn.silu(pre_back)
    grad_back = upstream * slope(pre_back)
    gmix_back = jnp.einsum("owt,cwt->oc", grad_back, taps_back, precision=lax.Precision.HIGHEST)
    gbias_back = jnp.sum(grad_back, axis=(1, 2))
    under_back = jnp.einsum("oc,owt->cwt", mixing_back, grad_back, precision=lax.Precision.HIGHEST)
    gkern_back = tap_grads(under_back, padded_act)
    into_front = depthwise(
        spread(under_back, kernel_extent, 1), kernel_back[:, ::-1, ::-1], row_count, column_count
    )
    grad_front = into_front * slope(pre_front)
    gmix_front = jnp.einsum("owt,cwt->oc", grad_front, taps_front, precision=lax.Precision.HIGHEST)
    gbias_front = jnp.sum(grad_front, axis=(1, 2))
    under_front = jnp.einsum(
        "oc,owt->cwt", mixing_front, grad_front, precision=lax.Precision.HIGHEST
    )
    gkern_front = tap_grads(under_front, padded_in)
    signal_grad = depthwise(
        spread(under_front, kernel_extent, 1), kernel_front[:, ::-1, ::-1], row_count, column_count
    )
    totals = (gkern_front, gmix_front, gbias_front, gkern_back, gmix_back, gbias_back)
    packed = jnp.concatenate([item.reshape(-1) for item in totals])
    for group in REDUCTION_ORDER:
        packed = lax.psum(packed, group)
    sizes = [math.prod(item.shape) for item in totals]
    pieces = jnp.split(packed, [sum(sizes[: k + 1]) for k in range(len(sizes) - 1)])
    totals = [piece.reshape(item.shape) for piece, item in zip(pieces, totals)]
    factor = 1.0 / math.sqrt(
        row_count * lax.axis_size(WIRE) * column_count * lax.axis_size(TICK)
    )
    return (
        response,
        signal_grad,
        totals[0] * factor,
        totals[1] * factor,
        totals[2] * factor,
        totals[3] * factor,
        totals[4] * factor,
        totals[5] * factor,
    )


def solution(mesh):
    fine = Mesh(mesh.devices.reshape(8, 4, 2, 2, 4), TICK + WIRE)
    block = P(None, WIRE, TICK)
    in_specs = (block, P(), P(), P(), P(), P(), P(), block)
    out_specs = (block, block, P(), P(), P(), P(), P(), P())
    return jax.shard_map(
        per_device, mesh=fine, in_specs=in_specs, out_specs=out_specs, check_vma=False
    )
```

```python
import math

import jax
import jax.numpy as jnp
from jax import lax
from jax.experimental import pallas as pl
from jax.experimental.pallas import tpu as pltpu
from jax.sharding import Mesh, PartitionSpec as P

TICK = ("y", "z_hi", "core")
WIRE = ("z_lo", "x")
REDUCTION_ORDER = ("core", "x", ("z_hi", "z_lo"), "y")

CHANNELS, WIRES, TICKS = 16, 64, 128
STEP = 8
BLOCKS = TICKS // STEP
MARGIN = 4
ROWS = WIRES + 2 * MARGIN
FIRST = 8
OWN = FIRST + MARGIN
DEEP = FIRST + ROWS + 8
TILE = 128
F32, BF16 = jnp.float32, jnp.bfloat16


def lanes(shape):
    return lax.broadcasted_iota(jnp.int32, shape, len(shape) - 1)


def exchange(tiles):
    tiles = list(tiles)
    lane = lanes(tiles[0].shape)
    for bit in range(4):
        shift = STEP << bit
        upper = (lane & shift) != 0
        for low in range(16):
            if low >> bit & 1:
                continue
            high = low | 1 << bit
            a, b = tiles[low], tiles[high]
            tiles[low] = jnp.where(upper, pltpu.roll(b, shift, 1), a)
            tiles[high] = jnp.where(upper, b, pltpu.roll(a, TILE - shift, 1))
    return tiles


def tap(row, column, flip):
    return (2 - row) * 9 + 8 - column if flip else row * 9 + column


def convolve(source, target, kernel, flip, planes, first, groups):
    def group(index, _):
        base = first + 8 * index
        weights = [[kernel[tap(i, j, flip)] for j in range(9)] for i in range(3)]
        sums = {}
        for at in range(planes + 8):
            rows = [source[at, pl.ds(base + i - 1, 8), :] for i in range(3)]
            for j in range(9):
                plane = at - j
                if not 0 <= plane < planes:
                    continue
                value = weights[0][j] * rows[0] + weights[1][j] * rows[1] + weights[2][j] * rows[2]
                sums[plane] = sums[plane] + value if j else value
                if j == 8:
                    target[plane, pl.ds(base, 8), :] = sums.pop(plane)
        return 0

    lax.fori_loop(0, groups, group, 0)


def correlate(upward, ahead, source, start, lines, place):
    def group(index, carry):
        base = OWN + 8 * index
        sums = list(carry)
        ups = {}
        for at in range(BLOCKS + 8):
            if at < BLOCKS:
                ups[at] = upward[ahead + at, pl.ds(base, 8), :]
            rows = [source[start + at, pl.ds(base + i - 1, 8), :] for i in range(3)]
            for j in range(9):
                if 0 <= at - j < BLOCKS:
                    for i in range(3):
                        sums[9 * i + j] = sums[9 * i + j] + ups[at - j] * rows[i]
        return tuple(sums)

    zero = tuple(jnp.zeros((8, TILE), F32) for _ in range(27))
    sums = lax.fori_loop(0, WIRES // 8, group, zero)
    for k in range(27):
        lines[place + k : place + k + 1, :] = jnp.sum(sums[k], axis=0, keepdims=True)


def split(value):
    high = value.astype(BF16)
    return high, (value - high.astype(F32)).astype(BF16)


def mix(value, matrix):
    both = jnp.dot(jnp.concatenate(split(value), axis=1), matrix, preferred_element_type=F32)
    return both[:, :TILE] + both[:, TILE:]


def outer(left, right):
    lh, ll = split(left)
    rh, rl = split(right)
    return lax.dot_general(
        jnp.concatenate([lh, lh, ll], axis=0),
        jnp.concatenate([rh, rl, rh], axis=0),
        (((0,), (0,)), ((), ())),
        preferred_element_type=F32,
    )


def exact(left, right, contract):
    return lax.dot_general(
        left,
        right,
        (contract, ((), ())),
        precision=lax.Precision.HIGHEST,
        preferred_element_type=F32,
    )


def body(
    place, s_own, s_low, s_high, u_own, u_low, u_high, h_up, h_down, c_low, c_high,
    taps_front, taps_back, mixings, offsets,
    response, signal_grad, sums,
    sig, ups, fields_f, act, slope, fields_b, grads, u_back, u_front, result,
    kernel_front, kernel_back, halves, lines,
):
    tick_at, wire_at = place[0], place[1]

    spread = (lanes((CHANNELS, TILE)) // STEP) == lax.broadcasted_iota(
        jnp.int32, (CHANNELS, TILE), 0
    )
    spread = jnp.where(spread, 1.0, 0.0)
    for kernel, raw in ((kernel_front, taps_front), (kernel_back, taps_back)):
        wide = exact(raw[...], spread, ((0,), (0,)))
        for k in range(27):
            kernel[k] = jnp.broadcast_to(wide[k : k + 1, :], (8, TILE))
    biases = exact(offsets[...], spread, ((1,), (0,)))
    same = (lanes((TILE, TILE)) % STEP) == (
        lax.broadcasted_iota(jnp.int32, (TILE, TILE), 0) % STEP
    )
    for k in range(4):
        wide = exact(exact(spread, mixings[k], ((0,), (0,))), spread, ((1,), (0,)))
        high, low = split(jnp.where(same, wide, 0.0))
        halves[k, 0:TILE, 0:TILE] = high
        halves[k, 0:TILE, TILE:] = low
        halves[k, TILE:, 0:TILE] = high
        halves[k, TILE:, TILE:] = jnp.zeros((TILE, TILE), BF16)

    pad = jnp.zeros((8, TILE), F32)
    for planes in (sig, act, u_back, u_front):

        def clear(at, _, planes=planes):
            planes[at, 0:FIRST, :] = pad
            planes[at, FIRST + ROWS : DEEP, :] = pad
            return 0

        lax.fori_loop(0, planes.shape[0], clear, 0)
    lines[...] = jnp.zeros_like(lines)

    def load(source, row):
        return exchange([source[c, pl.ds(row, 8), :] for c in range(CHANNELS)])

    def fill(group, _):
        row = pl.multiple_of(8 * group, 8)
        for source, target, start in (
            (s_low, sig, 0),
            (s_own, sig, BLOCKS),
            (s_high, sig, 2 * BLOCKS),
            (u_own, ups, BLOCKS // 2),
        ):
            for a, tile in enumerate(load(source, row)):
                target[start + a, pl.ds(OWN + row, 8), :] = tile
        return 0

    lax.fori_loop(0, WIRES // 8, fill, 0)

    def fill_packed(group, _):
        row = pl.multiple_of(8 * group, 8)
        for source, start in ((u_low, 0), (u_high, BLOCKS // 2 + BLOCKS)):
            for a, tile in enumerate(load(source, row)):
                second, plane = divmod(a, BLOCKS // 2)
                at = OWN + row + second * (WIRES // 2)
                ups[start + plane, pl.ds(at, 8), :] = tile
        return 0

    lax.fori_loop(0, WIRES // 16, fill_packed, 0)
    for base, strips in (
        (FIRST, (c_low.at[0], h_up, c_high.at[0])),
        (OWN + WIRES, (c_low.at[1], h_down, c_high.at[1])),
    ):
        for k, strip in enumerate(strips):
            for a, tile in enumerate(load(strip, 0)):
                sig[BLOCKS * k + a, base : base + MARGIN, :] = tile[0:MARGIN]
                plane = BLOCKS * k + a - BLOCKS // 2
                if 0 <= plane < 2 * BLOCKS:
                    ups[plane, base : base + MARGIN, :] = tile[MARGIN:]

    whole = pl.ds(FIRST, ROWS)

    def rows_of(planes, at):
        return planes[pl.ds(at, 2), whole, :].reshape(2 * ROWS, TILE)

    def put(planes, at, value):
        planes[pl.ds(at, 2), whole, :] = value.reshape(2, ROWS, TILE)

    convolve(sig, fields_f, kernel_front, False, 40, FIRST, ROWS // 8)
    order = lax.broadcasted_iota(jnp.int32, (2 * ROWS, TILE), 0)
    wire = jnp.where(order < ROWS, order, order - ROWS) - MARGIN
    wire_in = jnp.logical_and(
        jnp.logical_or(wire >= 0, wire_at > 0), jnp.logical_or(wire < WIRES, wire_at < 7)
    )

    def front(pair, _):
        at = 2 * pair
        value = mix(rows_of(fields_f, at), halves[0]) + biases[0:1, :]
        tick_in = jnp.logical_and(
            jnp.logical_or(at >= 12, tick_at > 0), jnp.logical_or(at < 28, tick_at < 63)
        )
        inside = jnp.logical_and(wire_in, tick_in)
        sigmoid = 1.0 / (1.0 + jnp.exp(-value))
        put(act, at, jnp.where(inside, value * sigmoid, 0.0))
        put(slope, at, jnp.where(inside, sigmoid * (1.0 + value * (1.0 - sigmoid)), 0.0))
        return 0

    lax.fori_loop(0, 20, front, 0)

    convolve(act, fields_b, kernel_back, False, 32, FIRST, ROWS // 8)

    def back(pair, _):
        at = 2 * pair
        value = mix(rows_of(fields_b, at), halves[1]) + biases[1:2, :]
        sigmoid = 1.0 / (1.0 + jnp.exp(-value))
        put(result, at, value * sigmoid)
        grad = rows_of(ups, at) * (sigmoid * (1.0 + value * (1.0 - sigmoid)))
        put(grads, at, grad)
        put(u_back, at, mix(grad, halves[2]))
        return 0

    lax.fori_loop(0, 16, back, 0)

    def give(target, start):
        def some(group, _):
            row = pl.multiple_of(8 * group, 8)
            tiles = [result[start + a, pl.ds(OWN + row, 8), :] for a in range(BLOCKS)]
            for c, tile in enumerate(exchange(tiles)):
                target[c, pl.ds(row, 8), :] = tile
            return 0

        lax.fori_loop(0, WIRES // 8, some, 0)

    def tally(ahead, fields, start, square_at, line_at):
        own = pl.ds(OWN, WIRES)

        def some(pair, carry):
            square, line = carry
            grad = grads[pl.ds(ahead + 2 * pair, 2), own, :].reshape(2 * WIRES, TILE)
            field = fields[pl.ds(start + 2 * pair, 2), own, :].reshape(2 * WIRES, TILE)
            line = line + jnp.sum(grad.reshape(2 * WIRES // 8, 8, TILE), axis=0)
            return square + outer(grad, field), line

        square, line = lax.fori_loop(
            0, BLOCKS // 2, some, (jnp.zeros((TILE, TILE), F32), jnp.zeros((8, TILE), F32))
        )
        square = jnp.where(same, square, 0.0).reshape(CHANNELS, STEP, TILE)
        lines[square_at : square_at + CHANNELS, :] = jnp.sum(square, axis=1)
        lines[line_at : line_at + 1, :] = jnp.sum(line, axis=0, keepdims=True)

    give(response, 8)
    tally(8, fields_b, 8, 64, 27)
    correlate(u_back, 8, act, 8, lines, 0)

    convolve(u_back, fields_b, kernel_back, True, 24, FIRST, ROWS // 8)

    def under_front(pair, _):
        at = 2 * pair
        grad = rows_of(fields_b, at) * rows_of(slope, at + 8)
        put(grads, at, grad)
        put(u_front, at, mix(grad, halves[3]))
        return 0

    lax.fori_loop(0, 12, under_front, 0)
    tally(4, fields_f, 12, 80, 59)
    correlate(u_front, 4, sig, 12, lines, 32)
    convolve(u_front, result, kernel_front, True, 16, OWN, WIRES // 8)
    give(signal_grad, 0)

    found = lines[...]
    for shift in (1, 2, 4):
        found = found + pltpu.roll(found, TILE - shift, 1)
    row = lax.broadcasted_iota(jnp.int32, (8, TILE), 0)
    for k in range(12):
        turned = pltpu.roll(found[8 * k : 8 * k + 8], 0, 1, stride=1, stride_axis=0)
        sums[k : k + 1, :] = jnp.sum(
            jnp.where(lanes((8, TILE)) % STEP == row, turned, 0.0), axis=0, keepdims=True
        )


def local(*arrays, interpret=False):
    vmem = pl.BlockSpec(memory_space=pltpu.VMEM)
    field = jax.ShapeDtypeStruct((CHANNELS, WIRES, TICKS), F32)
    planes = lambda count: pltpu.VMEM((count, DEEP, TILE), F32)
    return pl.pallas_call(
        body,
        out_shape=(field, field, jax.ShapeDtypeStruct((12, TILE), F32)),
        in_specs=[pl.BlockSpec(memory_space=pltpu.SMEM)] + [vmem] * (len(arrays) - 1),
        out_specs=(vmem, vmem, vmem),
        scratch_shapes=[
            planes(48),
            planes(32),
            planes(40),
            planes(40),
            planes(40),
            planes(32),
            planes(32),
            planes(32),
            planes(24),
            planes(32),
            pltpu.VMEM((27, 8, TILE), F32),
            pltpu.VMEM((27, 8, TILE), F32),
            pltpu.VMEM((4, 2 * TILE, 2 * TILE), BF16),
            pltpu.VMEM((96, TILE), F32),
        ],
        compiler_params=pltpu.CompilerParams(vmem_limit_bytes=48 * 1024 * 1024),
        interpret=interpret,
        name="blocks",
    )(*arrays)


def shift(value, axes, step):
    count = lax.axis_size(axes)
    pairs = [(i, i + step) for i in range(count) if 0 <= i + step < count]
    return lax.ppermute(value, axes, pairs)


def per_device(
    signal,
    kernel_front,
    mixing_front,
    offset_front,
    kernel_back,
    mixing_back,
    offset_back,
    upstream,
):
    s_low, s_high = shift(signal, TICK, 1), shift(signal, TICK, -1)
    strip_down = jnp.concatenate([signal[:, WIRES - 4 :], upstream[:, WIRES - 4 :]], axis=1)
    strip_up = jnp.concatenate([signal[:, :4], upstream[:, :4]], axis=1)
    h_up, h_down = shift(strip_down, WIRE, 1), shift(strip_up, WIRE, -1)
    pack = lambda part: jnp.concatenate([part[:, : WIRES // 2], part[:, WIRES // 2 :]], axis=2)
    u_low = shift(pack(upstream[:, :, 64:]), TICK, 1)
    u_high = shift(pack(upstream[:, :, :64]), TICK, -1)
    corner = jnp.stack([h_up, h_down])
    c_low, c_high = shift(corner, TICK, 1), shift(corner, TICK, -1)
    place = jnp.stack([lax.axis_index(TICK), lax.axis_index(WIRE)]).astype(jnp.int32)
    response, signal_grad, sums = local(
        place,
        *(signal, s_low, s_high, upstream, u_low, u_high, h_up, h_down, c_low, c_high),
        kernel_front.reshape(CHANNELS, 27),
        kernel_back.reshape(CHANNELS, 27),
        jnp.stack([mixing_front.T, mixing_back.T, mixing_back, mixing_front]),
        jnp.stack([offset_front, offset_back]),
    )
    for group in REDUCTION_ORDER:
        sums = lax.psum(sums, group)
    factor = 1.0 / math.sqrt(WIRES * lax.axis_size(WIRE) * TICKS * lax.axis_size(TICK))
    rows = (sums * factor).reshape(12, CHANNELS, STEP).transpose(0, 2, 1).reshape(96, CHANNELS)
    taps_of = lambda first: rows[first : first + 27].T.reshape(CHANNELS, 3, 9)
    return (
        response,
        signal_grad,
        taps_of(32),
        rows[80:96],
        rows[59],
        taps_of(0),
        rows[64:80],
        rows[27],
    )


def solution(mesh):
    fine = Mesh(mesh.devices.reshape(8, 4, 2, 2, 4), TICK + WIRE)
    block = P(None, WIRE, TICK)
    in_specs = (block, P(), P(), P(), P(), P(), P(), block)
    out_specs = (block, block, P(), P(), P(), P(), P(), P())
    return jax.shard_map(
        per_device, mesh=fine, in_specs=in_specs, out_specs=out_specs, check_vma=False
    )
```

```python
import math

import jax
import jax.numpy as jnp
from jax import lax
from jax.experimental import pallas as pl
from jax.experimental.pallas import tpu as pltpu
from jax.sharding import Mesh, PartitionSpec as P

TICK = ("y", "z_hi", "core")
WIRE = ("z_lo", "x")
REDUCTION_ORDER = ("core", "x", ("z_hi", "z_lo"), "y")

CHANNELS, WIRES, TICKS = 16, 64, 128
STEP = 8
BLOCKS = TICKS // STEP
MARGIN = 4
OWN = 12
DEEP = 88
PACK = WIRES // 2
TILE = 128
F32, BF16 = jnp.float32, jnp.bfloat16


def lanes(shape):
    return lax.broadcasted_iota(jnp.int32, shape, len(shape) - 1)


def exchange(tiles):
    tiles = list(tiles)
    lane = lanes(tiles[0].shape)
    for bit in range(4):
        shift = STEP << bit
        upper = (lane & shift) != 0
        for low in range(16):
            if low >> bit & 1:
                continue
            high = low | 1 << bit
            a, b = tiles[low], tiles[high]
            tiles[low] = jnp.where(upper, pltpu.roll(b, shift, 1), a)
            tiles[high] = jnp.where(upper, b, pltpu.roll(a, TILE - shift, 1))
    return tiles


def tap(row, column, flip):
    return (2 - row) * 9 + 8 - column if flip else row * 9 + column


def convolve(source, target, kernel, flip, planes, first, last):
    def group(index, _):
        base = OWN + jnp.minimum(first + 8 * index, last - 8)
        weights = [[kernel[tap(i, j, flip)] for j in range(9)] for i in range(3)]
        sums = {}
        for at in range(planes + 8):
            rows = [source[at, pl.ds(base + i - 1, 8), :] for i in range(3)]
            for j in range(9):
                plane = at - j
                if not 0 <= plane < planes:
                    continue
                value = weights[0][j] * rows[0] + weights[1][j] * rows[1] + weights[2][j] * rows[2]
                sums[plane] = sums[plane] + value if j else value
                if j == 8:
                    target[plane, pl.ds(base, 8), :] = sums.pop(plane)
        return 0

    lax.fori_loop(0, (last - first + 7) // 8, group, 0)


def correlate(upward, ahead, source, start, lines, place):
    def group(index, carry):
        base = OWN + 8 * index
        sums = list(carry)
        ups = {}
        for at in range(BLOCKS + 8):
            if at < BLOCKS:
                ups[at] = upward[ahead + at, pl.ds(base, 8), :]
            rows = [source[start + at, pl.ds(base + i - 1, 8), :] for i in range(3)]
            for j in range(9):
                if 0 <= at - j < BLOCKS:
                    for i in range(3):
                        sums[9 * i + j] = sums[9 * i + j] + ups[at - j] * rows[i]
        return tuple(sums)

    zero = tuple(jnp.zeros((8, TILE), F32) for _ in range(27))
    sums = lax.fori_loop(0, WIRES // 8, group, zero)
    for k in range(27):
        lines[place + k : place + k + 1, :] = jnp.sum(sums[k], axis=0, keepdims=True)


def split(value):
    high = value.astype(BF16)
    return high, (value - high.astype(F32)).astype(BF16)


def mix(value, matrix):
    both = jnp.dot(jnp.concatenate(split(value), axis=1), matrix, preferred_element_type=F32)
    return both[:, :TILE] + both[:, TILE:]


def outer(left, right):
    lh, ll = split(left)
    rh, rl = split(right)
    return lax.dot_general(
        jnp.concatenate([lh, lh, ll], axis=0),
        jnp.concatenate([rh, rl, rh], axis=0),
        (((0,), (0,)), ((), ())),
        preferred_element_type=F32,
    )


def exact(left, right, contract):
    return lax.dot_general(
        left,
        right,
        (contract, ((), ())),
        precision=lax.Precision.HIGHEST,
        preferred_element_type=F32,
    )


PLANES = dict(
    sig=48, ups=32, fields_f=40, act=40, slope=40, fields_b=32, grads_b=32, u_back=32, result=32,
    grads_f=24, u_front=24, back_out=16,
)


def load(source, row):
    return exchange([source[c, pl.ds(row, 8), :] for c in range(CHANNELS)])


class Stages:
    def __init__(self, held, halves, biases, place):
        self.__dict__.update(held)
        self.halves, self.biases, self.place = halves, biases, place

    def front(self, at, count, wire, wires, margin):
        rows = pl.ds(OWN + wire, wires)
        value = self.fields_f[pl.ds(at, count), rows, :].reshape(count * wires, TILE)
        value = mix(value, self.halves[0]) + self.biases[0:1, :]
        order = lax.broadcasted_iota(jnp.int32, (count, wires, TILE), 0)
        tick_at, wire_at = self.place[0], self.place[1]
        plane = at + order
        inside = jnp.logical_and(
            jnp.logical_or(plane >= 12, tick_at > 0), jnp.logical_or(plane < 28, tick_at < 63)
        )
        if margin:
            line = wire + lax.broadcasted_iota(jnp.int32, (count, wires, TILE), 1)
            inside = jnp.logical_and(
                inside,
                jnp.logical_and(
                    jnp.logical_or(line >= 0, wire_at > 0),
                    jnp.logical_or(line < WIRES, wire_at < 7),
                ),
            )
        sigmoid = 1.0 / (1.0 + jnp.exp(-value))
        act = (value * sigmoid).reshape(count, wires, TILE)
        slope = (sigmoid * (1.0 + value * (1.0 - sigmoid))).reshape(count, wires, TILE)
        self.act[pl.ds(at, count), rows, :] = jnp.where(inside, act, 0.0)
        self.slope[pl.ds(at, count), rows, :] = jnp.where(inside, slope, 0.0)

    def back(self, at, count, wire, wires):
        rows = pl.ds(OWN + wire, wires)
        here = lambda planes: planes[pl.ds(at, count), rows, :].reshape(count * wires, TILE)
        value = mix(here(self.fields_b), self.halves[1]) + self.biases[1:2, :]
        sigmoid = 1.0 / (1.0 + jnp.exp(-value))
        grad = here(self.ups) * (sigmoid * (1.0 + value * (1.0 - sigmoid)))
        under = mix(grad, self.halves[2])
        for planes, field in (
            (self.result, value * sigmoid), (self.grads_b, grad), (self.u_back, under)
        ):
            planes[pl.ds(at, count), rows, :] = field.reshape(count, wires, TILE)

    def under_front(self, fields, at, count, wire, wires):
        rows = pl.ds(OWN + wire, wires)
        grad = fields[pl.ds(at, count), rows, :] * self.slope[pl.ds(at + 8, count), rows, :]
        under = mix(grad.reshape(count * wires, TILE), self.halves[3])
        self.grads_f[pl.ds(at, count), rows, :] = grad
        self.u_front[pl.ds(at, count), rows, :] = under.reshape(count, wires, TILE)


def loop(count, step, unroll):
    def one(index, _):
        step(index)
        return 0

    lax.fori_loop(0, count, one, 0, unroll=unroll)


def inner(place, s_own, u_own, low, high, taps_front, taps_back, mixings, offsets, *rest):
    held = dict(zip(PLANES, rest))
    kernel_front, kernel_back, halves, biases, fields_d = rest[len(PLANES) :]

    spread = (lanes((CHANNELS, TILE)) // STEP) == lax.broadcasted_iota(
        jnp.int32, (CHANNELS, TILE), 0
    )
    spread = jnp.where(spread, 1.0, 0.0)
    for kernel, raw in ((kernel_front, taps_front), (kernel_back, taps_back)):
        wide = exact(raw[...], spread, ((0,), (0,)))
        for k in range(27):
            kernel[k] = jnp.broadcast_to(wide[k : k + 1, :], (8, TILE))
    biases[...] = exact(offsets[...], spread, ((1,), (0,)))
    same = (lanes((TILE, TILE)) % STEP) == (
        lax.broadcasted_iota(jnp.int32, (TILE, TILE), 0) % STEP
    )
    for k in range(4):
        wide = exact(exact(spread, mixings[k], ((0,), (0,))), spread, ((1,), (0,)))
        upper, lower = split(jnp.where(same, wide, 0.0))
        halves[k, 0:TILE, 0:TILE] = upper
        halves[k, 0:TILE, TILE:] = lower
        halves[k, TILE:, 0:TILE] = upper
        halves[k, TILE:, TILE:] = jnp.zeros((TILE, TILE), BF16)

    sig, ups = held["sig"], held["ups"]

    def fill(group):
        row = pl.multiple_of(8 * group, 8)
        for source, target, start in (
            (low, sig, 0),
            (s_own, sig, BLOCKS),
            (high, sig, 2 * BLOCKS),
            (u_own, ups, BLOCKS // 2),
        ):
            for a, tile in enumerate(load(source, row)):
                target[start + a, pl.ds(OWN + row, 8), :] = tile

    loop(WIRES // 8, fill, 1)

    def fill_packed(group):
        row = pl.multiple_of(8 * group, 8)
        for source, start in ((low, 0), (high, BLOCKS // 2 + BLOCKS)):
            for a, tile in enumerate(load(source, WIRES + row)):
                second, plane = divmod(a, BLOCKS // 2)
                ups[start + plane, pl.ds(OWN + row + second * PACK, 8), :] = tile

    loop(PACK // 8, fill_packed, 1)

    do = Stages(held, halves, biases, place)
    convolve(sig, do.fields_f, kernel_front, False, 40, 1, 63)
    loop(20, lambda k: do.front(2 * k, 2, 0, WIRES, False), 10)
    convolve(do.act, do.fields_b, kernel_back, False, 32, 2, 62)
    loop(16, lambda k: do.back(2 * k, 2, 0, WIRES), 8)
    convolve(do.u_back, fields_d, kernel_back, True, 24, 3, 61)
    loop(12, lambda k: do.under_front(fields_d, 2 * k, 2, 0, WIRES), 6)
    convolve(do.u_front, do.back_out, kernel_front, True, 16, 4, 60)


def border(place, h_up, h_down, *rest):
    many = len(PLANES) + 4
    response, signal_grad, sums = rest[many : many + 3]
    held = dict(zip(PLANES, rest[many + 3 :]))
    kernel_front, kernel_back, halves, biases = rest[len(PLANES) : many]
    fields_d, lines = rest[many + 3 + len(PLANES) :]
    do = Stages(held, halves, biases, place)
    sig, ups = do.sig, do.ups

    for second, base, strip in ((1, OWN - MARGIN, h_up), (0, OWN + WIRES, h_down)):
        pairs = [load(strip, 8 * k) for k in range(3)]
        for a in range(BLOCKS):
            sig[a, base : base + MARGIN, :] = pairs[0][a][:MARGIN]
            sig[BLOCKS + a, base : base + MARGIN, :] = pairs[0][a][MARGIN:]
            sig[2 * BLOCKS + a, base : base + MARGIN, :] = pairs[1][a][:MARGIN]
            ups[BLOCKS // 2 + a, base : base + MARGIN, :] = pairs[1][a][MARGIN:]
            plane = a - second * (BLOCKS // 2)
            if 0 <= plane < BLOCKS // 2:
                ups[plane, base : base + MARGIN, :] = pairs[2][a][:MARGIN]
                ups[BLOCKS // 2 + BLOCKS + plane, base : base + MARGIN, :] = pairs[2][a][MARGIN:]

    for start in (-3, 59):
        convolve(sig, do.fields_f, kernel_front, False, 40, start, start + 8)
    for start in (-3, 59):
        do.front(0, 40, start, 8, True)
    for start in (-2, 58):
        convolve(do.act, do.fields_b, kernel_back, False, 32, start, start + 8)
    for start in (-2, 58):
        do.back(0, 32, start, 8)
    for start in (-1, 57):
        convolve(do.u_back, fields_d, kernel_back, True, 24, start, start + 8)
    for start in (-1, 57):
        do.under_front(fields_d, 0, 24, start, 8)
    for start in (0, 56):
        convolve(do.u_front, do.back_out, kernel_front, True, 16, start, start + 8)

    lines[...] = jnp.zeros_like(lines)
    same = (lanes((TILE, TILE)) % STEP) == (
        lax.broadcasted_iota(jnp.int32, (TILE, TILE), 0) % STEP
    )

    def give(group):
        row = pl.multiple_of(8 * group, 8)
        for source, start, target in ((do.result, 8, response), (do.back_out, 0, signal_grad)):
            tiles = [source[start + a, pl.ds(OWN + row, 8), :] for a in range(BLOCKS)]
            for c, tile in enumerate(exchange(tiles)):
                target[c, pl.ds(row, 8), :] = tile

    loop(WIRES // 8, give, 1)

    def tally(grads, ahead, fields, start, square_at, line_at):
        own = pl.ds(OWN, WIRES)

        def some(pair, carry):
            square, line = carry
            grad = grads[pl.ds(ahead + 2 * pair, 2), own, :].reshape(2 * WIRES, TILE)
            field = fields[pl.ds(start + 2 * pair, 2), own, :].reshape(2 * WIRES, TILE)
            line = line + jnp.sum(grad.reshape(2 * WIRES // 8, 8, TILE), axis=0)
            return square + outer(grad, field), line

        square, line = lax.fori_loop(
            0,
            BLOCKS // 2,
            some,
            (jnp.zeros((TILE, TILE), F32), jnp.zeros((8, TILE), F32)),
            unroll=8,
        )
        square = jnp.where(same, square, 0.0).reshape(CHANNELS, STEP, TILE)
        lines[square_at : square_at + CHANNELS, :] = jnp.sum(square, axis=1)
        lines[line_at : line_at + 1, :] = jnp.sum(line, axis=0, keepdims=True)

    tally(do.grads_b, 8, do.fields_b, 8, 64, 27)
    tally(do.grads_f, 4, do.fields_f, 12, 80, 59)
    correlate(do.u_back, 8, do.act, 8, lines, 0)
    correlate(do.u_front, 4, sig, 12, lines, 32)

    found = lines[...]
    for step in (1, 2, 4):
        found = found + pltpu.roll(found, TILE - step, 1)
    row = lax.broadcasted_iota(jnp.int32, (8, TILE), 0)
    for k in range(12):
        turned = pltpu.roll(found[8 * k : 8 * k + 8], 0, 1, stride=1, stride_axis=0)
        sums[k : k + 1, :] = jnp.sum(
            jnp.where(lanes((8, TILE)) % STEP == row, turned, 0.0), axis=0, keepdims=True
        )


VMEM = pl.BlockSpec(memory_space=pltpu.VMEM)
SMEM = pl.BlockSpec(memory_space=pltpu.SMEM)
SIZES = dict(compiler_params=pltpu.CompilerParams(vmem_limit_bytes=24 * 1024 * 1024))
HELD = [jax.ShapeDtypeStruct((count, DEEP, TILE), F32) for count in PLANES.values()]


def call_inner(*arrays):
    tables = [
        jax.ShapeDtypeStruct((27, 8, TILE), F32),
        jax.ShapeDtypeStruct((27, 8, TILE), F32),
        jax.ShapeDtypeStruct((4, 2 * TILE, 2 * TILE), BF16),
        jax.ShapeDtypeStruct((2, TILE), F32),
    ]
    return pl.pallas_call(
        inner,
        out_shape=HELD + tables,
        in_specs=[SMEM] + [VMEM] * (len(arrays) - 1),
        out_specs=[VMEM] * (len(HELD) + 4),
        scratch_shapes=[pltpu.VMEM((24, DEEP, TILE), F32)],
        name="inner",
        **SIZES,
    )(*arrays)


def call_border(*arrays):
    field = jax.ShapeDtypeStruct((CHANNELS, WIRES, TICKS), F32)
    return pl.pallas_call(
        border,
        out_shape=[field, field, jax.ShapeDtypeStruct((12, TILE), F32)] + HELD,
        in_specs=[SMEM] + [VMEM] * (len(arrays) - 1),
        out_specs=[VMEM] * (3 + len(HELD)),
        scratch_shapes=[
            pltpu.VMEM((24, DEEP, TILE), F32),
            pltpu.VMEM((96, TILE), F32),
        ],
        input_output_aliases={3 + k: 3 + k for k in range(len(HELD))},
        name="border",
        **SIZES,
    )(*arrays)[:3]


def shift(value, axes, step):
    count = lax.axis_size(axes)
    pairs = [(i, i + step) for i in range(count) if 0 <= i + step < count]
    return lax.ppermute(value, axes, pairs)


def per_device(
    signal,
    kernel_front,
    mixing_front,
    offset_front,
    kernel_back,
    mixing_back,
    offset_back,
    upstream,
):
    pack = lambda part: jnp.concatenate([part[:, :PACK], part[:, PACK:]], axis=2)
    join = lambda *parts: jnp.concatenate(parts, axis=1)
    low = shift(join(signal, pack(upstream[:, :, 64:])), TICK, 1)
    high = shift(join(signal, pack(upstream[:, :, :64])), TICK, -1)

    def strip(first, packed):
        rows = slice(first, first + MARGIN)
        halves = slice(packed, packed + MARGIN)
        return join(
            low[:, rows], signal[:, rows], high[:, rows], upstream[:, rows],
            low[:, halves], high[:, halves],
        )

    h_up = shift(strip(WIRES - MARGIN, WIRES + PACK - MARGIN), WIRE, 1)
    h_down = shift(strip(0, WIRES), WIRE, -1)
    place = jnp.stack([lax.axis_index(TICK), lax.axis_index(WIRE)]).astype(jnp.int32)
    held = call_inner(
        place,
        *(signal, upstream, low, high),
        kernel_front.reshape(CHANNELS, 27),
        kernel_back.reshape(CHANNELS, 27),
        jnp.stack([mixing_front.T, mixing_back.T, mixing_back, mixing_front]),
        jnp.stack([offset_front, offset_back]),
    )
    response, signal_grad, sums = call_border(place, h_up, h_down, *held)
    for group in REDUCTION_ORDER:
        sums = lax.psum(sums, group)
    factor = 1.0 / math.sqrt(WIRES * lax.axis_size(WIRE) * TICKS * lax.axis_size(TICK))
    rows = (sums * factor).reshape(12, CHANNELS, STEP).transpose(0, 2, 1).reshape(96, CHANNELS)
    taps_of = lambda first: rows[first : first + 27].T.reshape(CHANNELS, 3, 9)
    return (
        response,
        signal_grad,
        taps_of(32),
        rows[80:96],
        rows[59],
        taps_of(0),
        rows[64:80],
        rows[27],
    )


def solution(mesh):
    fine = Mesh(mesh.devices.reshape(8, 4, 2, 2, 4), TICK + WIRE)
    block = P(None, WIRE, TICK)
    in_specs = (block, P(), P(), P(), P(), P(), P(), block)
    out_specs = (block, block, P(), P(), P(), P(), P(), P())
    return jax.shard_map(
        per_device, mesh=fine, in_specs=in_specs, out_specs=out_specs, check_vma=False
    )
```

```python
import functools
import math

import jax
import jax.numpy as jnp
from jax import lax
from jax.experimental import pallas as pl
from jax.experimental.pallas import tpu as pltpu
from jax.sharding import Mesh, PartitionSpec as P

TICK = ("y", "z_hi", "core")
WIRE = ("z_lo", "x")
REDUCTION_ORDER = ("core", "x", ("z_hi", "z_lo"), "y")

CHANNELS, WIRES, TICKS = 16, 64, 128
STEP = 8
BLOCKS = TICKS // STEP
MARGIN = 4
OWN = 12
DEEP = 88
PACK = WIRES // 2
TILE = 128
F32, BF16 = jnp.float32, jnp.bfloat16


def lanes(shape):
    return lax.broadcasted_iota(jnp.int32, shape, len(shape) - 1)


def turn(tile, shift):
    return pltpu.roll(tile, shift, 1) if shift else tile


def exchange(tiles):
    lane = lanes(tiles[0].shape)
    tiles = [turn(tile, STEP * c) for c, tile in enumerate(tiles)]
    tiles = [tiles[-k % 16] for k in range(16)]
    for bit in range(4):
        upper = (lane & (STEP << bit)) != 0
        tiles = [jnp.where(upper, tiles[k - (1 << bit)], tiles[k]) for k in range(16)]
    return [turn(tile, (TILE - STEP * a) % TILE) for a, tile in enumerate(tiles)]


def tap(row, column, flip):
    return (2 - row) * 9 + 8 - column if flip else row * 9 + column


def convolve(source, target, kernel, flip, planes, first, last):
    def group(index, _):
        base = OWN + jnp.minimum(first + 8 * index, last - 8)
        weights = [[kernel[tap(i, j, flip)] for j in range(9)] for i in range(3)]
        sums = {}
        for at in range(planes + 8):
            rows = [source[at, pl.ds(base + i - 1, 8), :] for i in range(3)]
            for j in range(9):
                plane = at - j
                if not 0 <= plane < planes:
                    continue
                value = weights[0][j] * rows[0] + weights[1][j] * rows[1] + weights[2][j] * rows[2]
                sums[plane] = sums[plane] + value if j else value
                if j == 8:
                    target[plane, pl.ds(base, 8), :] = sums.pop(plane)
        return 0

    lax.fori_loop(0, (last - first + 7) // 8, group, 0)


def correlate(upward, ahead, source, start, lines, place):
    def group(index, carry):
        base = OWN + 8 * index
        sums = list(carry)
        ups = {}
        for at in range(BLOCKS + 8):
            if at < BLOCKS:
                ups[at] = upward[ahead + at, pl.ds(base, 8), :]
            rows = [source[start + at, pl.ds(base + i - 1, 8), :] for i in range(3)]
            for j in range(9):
                if 0 <= at - j < BLOCKS:
                    for i in range(3):
                        sums[9 * i + j] = sums[9 * i + j] + ups[at - j] * rows[i]
        return tuple(sums)

    zero = tuple(jnp.zeros((8, TILE), F32) for _ in range(27))
    sums = lax.fori_loop(0, WIRES // 8, group, zero)
    for k in range(27):
        lines[place + k : place + k + 1, :] = jnp.sum(sums[k], axis=0, keepdims=True)


def split(value):
    high = value.astype(BF16)
    return high, (value - high.astype(F32)).astype(BF16)


def mix(value, matrix):
    both = jnp.dot(jnp.concatenate(split(value), axis=1), matrix, preferred_element_type=F32)
    return both[:, :TILE] + both[:, TILE:]


def outer(left, right):
    lh, ll = split(left)
    rh, rl = split(right)
    return lax.dot_general(
        jnp.concatenate([lh, lh, ll], axis=0),
        jnp.concatenate([rh, rl, rh], axis=0),
        (((0,), (0,)), ((), ())),
        preferred_element_type=F32,
    )


def exact(left, right, contract):
    return lax.dot_general(
        left,
        right,
        (contract, ((), ())),
        precision=lax.Precision.HIGHEST,
        preferred_element_type=F32,
    )


PLANES = dict(
    sig=48, ups=32, fields_f=40, act=40, slope=40, fields_b=32, grads_b=32, u_back=32, result=32,
    grads_f=24, u_front=24, back_out=16,
)


def load(source, row):
    return exchange([source[c, pl.ds(row, 8), :] for c in range(CHANNELS)])


class Stages:
    def __init__(self, held, halves, biases, place):
        self.__dict__.update(held)
        self.halves, self.biases, self.place = halves, biases, place

    def front(self, at, count, wire, wires, margin):
        rows = pl.ds(OWN + wire, wires)
        value = self.fields_f[pl.ds(at, count), rows, :].reshape(count * wires, TILE)
        value = mix(value, self.halves[0]) + self.biases[0:1, :]
        order = lax.broadcasted_iota(jnp.int32, (count, wires, TILE), 0)
        tick_at, wire_at = self.place[0], self.place[1]
        plane = at + order
        inside = jnp.logical_and(
            jnp.logical_or(plane >= 12, tick_at > 0), jnp.logical_or(plane < 28, tick_at < 63)
        )
        if margin:
            line = wire + lax.broadcasted_iota(jnp.int32, (count, wires, TILE), 1)
            inside = jnp.logical_and(
                inside,
                jnp.logical_and(
                    jnp.logical_or(line >= 0, wire_at > 0),
                    jnp.logical_or(line < WIRES, wire_at < 7),
                ),
            )
        sigmoid = 1.0 / (1.0 + jnp.exp(-value))
        act = (value * sigmoid).reshape(count, wires, TILE)
        slope = (sigmoid * (1.0 + value * (1.0 - sigmoid))).reshape(count, wires, TILE)
        self.act[pl.ds(at, count), rows, :] = jnp.where(inside, act, 0.0)
        self.slope[pl.ds(at, count), rows, :] = jnp.where(inside, slope, 0.0)

    def back(self, at, count, wire, wires):
        rows = pl.ds(OWN + wire, wires)
        here = lambda planes: planes[pl.ds(at, count), rows, :].reshape(count * wires, TILE)
        value = mix(here(self.fields_b), self.halves[1]) + self.biases[1:2, :]
        sigmoid = 1.0 / (1.0 + jnp.exp(-value))
        grad = here(self.ups) * (sigmoid * (1.0 + value * (1.0 - sigmoid)))
        under = mix(grad, self.halves[2])
        for planes, field in (
            (self.result, value * sigmoid), (self.grads_b, grad), (self.u_back, under)
        ):
            planes[pl.ds(at, count), rows, :] = field.reshape(count, wires, TILE)

    def under_front(self, fields, at, count, wire, wires):
        rows = pl.ds(OWN + wire, wires)
        grad = fields[pl.ds(at, count), rows, :] * self.slope[pl.ds(at + 8, count), rows, :]
        under = mix(grad.reshape(count * wires, TILE), self.halves[3])
        self.grads_f[pl.ds(at, count), rows, :] = grad
        self.u_front[pl.ds(at, count), rows, :] = under.reshape(count, wires, TILE)


def loop(count, step, unroll):
    def one(index, _):
        step(index)
        return 0

    lax.fori_loop(0, count, one, 0, unroll=unroll)


def prepare(s_own, u_own, taps_front, taps_back, mixings, offsets, *rest):
    sig, kernel_front, kernel_back, halves, biases, own_up, own_down = rest
    for strip, rows in ((own_up, pl.ds(0, MARGIN)), (own_down, pl.ds(WIRES - MARGIN, MARGIN))):
        strip[:, :MARGIN, :] = s_own[:, rows, :]
        strip[:, MARGIN:, :] = u_own[:, rows, :]
    spread = (lanes((CHANNELS, TILE)) // STEP) == lax.broadcasted_iota(
        jnp.int32, (CHANNELS, TILE), 0
    )
    spread = jnp.where(spread, 1.0, 0.0)
    for kernel, raw in ((kernel_front, taps_front), (kernel_back, taps_back)):
        wide = exact(raw[...], spread, ((0,), (0,)))
        for k in range(27):
            kernel[k] = jnp.broadcast_to(wide[k : k + 1, :], (8, TILE))
    biases[...] = exact(offsets[...], spread, ((1,), (0,)))
    same = (lanes((TILE, TILE)) % STEP) == (
        lax.broadcasted_iota(jnp.int32, (TILE, TILE), 0) % STEP
    )
    for k in range(4):
        wide = exact(exact(spread, mixings[k], ((0,), (0,))), spread, ((1,), (0,)))
        upper, lower = split(jnp.where(same, wide, 0.0))
        halves[k, 0:TILE, 0:TILE] = upper
        halves[k, 0:TILE, TILE:] = lower
        halves[k, TILE:, 0:TILE] = upper
        halves[k, TILE:, TILE:] = jnp.zeros((TILE, TILE), BF16)

    def fill(group):
        row = pl.multiple_of(8 * group, 8)
        for a, tile in enumerate(load(s_own, row)):
            sig[BLOCKS + a, pl.ds(OWN + row, 8), :] = tile

    loop(WIRES // 8, fill, 1)


def cut(low, high, own_up, own_down, *rest):
    strip_up, strip_down = rest[5:7]
    slabs, arrived = rest[-2:]
    copies = []
    for k, row in enumerate((0, WIRES, WIRES - 8, WIRES + PACK - 8)):
        for side, source in enumerate((low, high)):
            at = 2 * k + side
            copies.append(
                pltpu.make_async_copy(
                    source.at[:, pl.ds(row, 8), :], slabs.at[at], arrived.at[at]
                )
            )
    for copy in copies:
        copy.start()
    for copy in copies:
        copy.wait()
    for strip, own, first, rows in (
        (strip_up, own_up, 0, slice(0, MARGIN)),
        (strip_down, own_down, 4, slice(MARGIN, 8)),
    ):
        strip[:, 0:8, :] = own[...]
        for k in range(4):
            strip[:, 8 + MARGIN * k : 8 + MARGIN * (k + 1), :] = slabs[first + k, :, rows, :]


def inner(place, low, high, u_own, *rest):
    kernel_front, kernel_back, halves, biases = rest[1:5]
    held = dict(zip(PLANES, rest[5:]))
    fields_d = rest[-1]
    sig, ups = held["sig"], held["ups"]

    def fill(group):
        row = pl.multiple_of(8 * group, 8)
        for source, target, start in (
            (low, sig, 0), (high, sig, 2 * BLOCKS), (u_own, ups, BLOCKS // 2)
        ):
            for a, tile in enumerate(load(source, row)):
                target[start + a, pl.ds(OWN + row, 8), :] = tile

    loop(WIRES // 8, fill, 1)

    def fill_packed(group):
        row = pl.multiple_of(8 * group, 8)
        for source, start in ((low, 0), (high, BLOCKS // 2 + BLOCKS)):
            for a, tile in enumerate(load(source, WIRES + row)):
                second, plane = divmod(a, BLOCKS // 2)
                ups[start + plane, pl.ds(OWN + row + second * PACK, 8), :] = tile

    loop(PACK // 8, fill_packed, 1)

    do = Stages(held, halves, biases, place)
    convolve(sig, do.fields_f, kernel_front, False, 40, 1, 63)
    loop(20, lambda k: do.front(2 * k, 2, 0, WIRES, False), 10)
    convolve(do.act, do.fields_b, kernel_back, False, 32, 2, 62)
    loop(16, lambda k: do.back(2 * k, 2, 0, WIRES), 8)
    convolve(do.u_back, fields_d, kernel_back, True, 24, 3, 61)
    loop(12, lambda k: do.under_front(fields_d, 2 * k, 2, 0, WIRES), 6)
    convolve(do.u_front, do.back_out, kernel_front, True, 16, 4, 60)


def border(place, h_up, h_down, *rest):
    many = len(PLANES) + 4
    response, signal_grad, sums = rest[many : many + 3]
    held = dict(zip(PLANES, rest[many + 3 :]))
    kernel_front, kernel_back, halves, biases = rest[len(PLANES) : many]
    fields_d, lines = rest[many + 3 + len(PLANES) :]
    do = Stages(held, halves, biases, place)
    sig, ups = do.sig, do.ups

    for second, base, strip in ((1, OWN - MARGIN, h_up), (0, OWN + WIRES, h_down)):
        pairs = [load(strip, 8 * k) for k in range(3)]
        for a in range(BLOCKS):
            sig[BLOCKS + a, base : base + MARGIN, :] = pairs[0][a][:MARGIN]
            ups[BLOCKS // 2 + a, base : base + MARGIN, :] = pairs[0][a][MARGIN:]
            sig[a, base : base + MARGIN, :] = pairs[1][a][:MARGIN]
            sig[2 * BLOCKS + a, base : base + MARGIN, :] = pairs[1][a][MARGIN:]
            plane = a - second * (BLOCKS // 2)
            if 0 <= plane < BLOCKS // 2:
                ups[plane, base : base + MARGIN, :] = pairs[2][a][:MARGIN]
                ups[BLOCKS // 2 + BLOCKS + plane, base : base + MARGIN, :] = pairs[2][a][MARGIN:]

    for start in (-3, 59):
        convolve(sig, do.fields_f, kernel_front, False, 40, start, start + 8)
    for start in (-3, 59):
        do.front(0, 40, start, 8, True)
    for start in (-2, 58):
        convolve(do.act, do.fields_b, kernel_back, False, 32, start, start + 8)
    for start in (-2, 58):
        do.back(0, 32, start, 8)
    for start in (-1, 57):
        convolve(do.u_back, fields_d, kernel_back, True, 24, start, start + 8)
    for start in (-1, 57):
        do.under_front(fields_d, 0, 24, start, 8)
    for start in (0, 56):
        convolve(do.u_front, do.back_out, kernel_front, True, 16, start, start + 8)

    lines[...] = jnp.zeros_like(lines)
    same = (lanes((TILE, TILE)) % STEP) == (
        lax.broadcasted_iota(jnp.int32, (TILE, TILE), 0) % STEP
    )

    def give(group):
        row = pl.multiple_of(8 * group, 8)
        for source, start, target in ((do.result, 8, response), (do.back_out, 0, signal_grad)):
            tiles = [source[start + a, pl.ds(OWN + row, 8), :] for a in range(BLOCKS)]
            for c, tile in enumerate(exchange(tiles)):
                target[c, pl.ds(row, 8), :] = tile

    loop(WIRES // 8, give, 1)

    def tally(grads, ahead, fields, start, square_at, line_at):
        own = pl.ds(OWN, WIRES)

        def some(pair, carry):
            square, line = carry
            grad = grads[pl.ds(ahead + 2 * pair, 2), own, :].reshape(2 * WIRES, TILE)
            field = fields[pl.ds(start + 2 * pair, 2), own, :].reshape(2 * WIRES, TILE)
            line = line + jnp.sum(grad.reshape(2 * WIRES // 8, 8, TILE), axis=0)
            return square + outer(grad, field), line

        square, line = lax.fori_loop(
            0,
            BLOCKS // 2,
            some,
            (jnp.zeros((TILE, TILE), F32), jnp.zeros((8, TILE), F32)),
            unroll=8,
        )
        square = jnp.where(same, square, 0.0).reshape(CHANNELS, STEP, TILE)
        lines[square_at : square_at + CHANNELS, :] = jnp.sum(square, axis=1)
        lines[line_at : line_at + 1, :] = jnp.sum(line, axis=0, keepdims=True)

    tally(do.grads_b, 8, do.fields_b, 8, 64, 27)
    tally(do.grads_f, 4, do.fields_f, 12, 80, 59)
    correlate(do.u_back, 8, do.act, 8, lines, 0)
    correlate(do.u_front, 4, sig, 12, lines, 32)

    found = lines[...]
    for step in (1, 2, 4):
        found = found + pltpu.roll(found, TILE - step, 1)
    row = lax.broadcasted_iota(jnp.int32, (8, TILE), 0)
    sums[12:16, :] = jnp.zeros((4, TILE), F32)
    for k in range(12):
        turned = pltpu.roll(found[8 * k : 8 * k + 8], 0, 1, stride=1, stride_axis=0)
        sums[k : k + 1, :] = jnp.sum(
            jnp.where(lanes((8, TILE)) % STEP == row, turned, 0.0), axis=0, keepdims=True
        )


VMEM = pl.BlockSpec(memory_space=pltpu.VMEM)
SMEM = pl.BlockSpec(memory_space=pltpu.SMEM)


def room(mebibytes):
    return pltpu.CompilerParams(vmem_limit_bytes=mebibytes * 1024 * 1024)


HELD = [jax.ShapeDtypeStruct((count, DEEP, TILE), F32) for count in PLANES.values()]


TABLES = [
    jax.ShapeDtypeStruct((27, 8, TILE), F32),
    jax.ShapeDtypeStruct((27, 8, TILE), F32),
    jax.ShapeDtypeStruct((4, 2 * TILE, 2 * TILE), BF16),
    jax.ShapeDtypeStruct((2, TILE), F32),
]


def call_prepare(*arrays):
    return pl.pallas_call(
        prepare,
        out_shape=HELD[:1] + TABLES + [jax.ShapeDtypeStruct((CHANNELS, 8, TICKS), F32)] * 2,
        in_specs=[VMEM] * len(arrays),
        out_specs=[VMEM] * 7,
        name="prepare",
        compiler_params=room(12),
    )(*arrays)


def call_cut(*arrays):
    strip = jax.ShapeDtypeStruct((CHANNELS, 24, TICKS), F32)
    return pl.pallas_call(
        cut,
        out_shape=[strip, strip] + HELD[:1] + TABLES,
        in_specs=[pl.BlockSpec(memory_space=pl.ANY)] * 2 + [VMEM] * (len(arrays) - 2),
        out_specs=[VMEM] * 7,
        scratch_shapes=[
            pltpu.VMEM((8, CHANNELS, 8, TICKS), F32),
            pltpu.SemaphoreType.DMA((8,)),
        ],
        input_output_aliases={4 + k: 2 + k for k in range(5)},
        name="cut",
        compiler_params=room(16),
    )(*arrays)


def call_inner(*arrays):
    return pl.pallas_call(
        inner,
        out_shape=HELD,
        in_specs=[SMEM] + [VMEM] * (len(arrays) - 1),
        out_specs=[VMEM] * len(HELD),
        scratch_shapes=[pltpu.VMEM((24, DEEP, TILE), F32)],
        input_output_aliases={4: 0},
        name="inner",
        compiler_params=room(24),
    )(*arrays)


def call_border(*arrays):
    field = jax.ShapeDtypeStruct((CHANNELS, WIRES, TICKS), F32)
    return pl.pallas_call(
        border,
        out_shape=[field, field, jax.ShapeDtypeStruct((16, TILE), F32)] + HELD,
        in_specs=[SMEM] + [VMEM] * (len(arrays) - 1),
        out_specs=[VMEM] * (3 + len(HELD)),
        scratch_shapes=[
            pltpu.VMEM((24, DEEP, TILE), F32),
            pltpu.VMEM((96, TILE), F32),
        ],
        input_output_aliases={3 + k: 3 + k for k in range(len(HELD))},
        name="border",
        compiler_params=room(24),
    )(*arrays)[:3]


def unpack(sums, front_taps, front_square, front_line, back_taps, back_square, back_line, factor):
    row = lax.broadcasted_iota(jnp.int32, (16, STEP, TILE), 1)
    wide = jnp.broadcast_to(sums[...][:, None, :], (16, STEP, TILE))
    wide = jnp.where(lanes(wide.shape) % STEP == row, wide, 0.0).reshape(16 * STEP, TILE)
    channel = lax.broadcasted_iota(jnp.int32, (TILE, CHANNELS), 0) // STEP
    pick = jnp.where(channel == lanes((TILE, CHANNELS)), 1.0, 0.0)
    rows = exact(wide, pick, ((1,), (0,))) * factor
    for taps, square, line, first, square_at, line_at in (
        (front_taps, front_square, front_line, 32, 80, 59),
        (back_taps, back_square, back_line, 0, 64, 27),
    ):
        for i in range(3):
            for j in range(9):
                at = first + 9 * i + j
                taps[j, i : i + 1, :] = rows[at : at + 1, :]
        square[...] = rows[square_at : square_at + CHANNELS, :]
        line[...] = rows[line_at : line_at + 1, :]


def call_unpack(sums, factor):
    shapes = [(9, 3, CHANNELS), (CHANNELS, CHANNELS), (1, CHANNELS)] * 2
    return pl.pallas_call(
        functools.partial(unpack, factor=factor),
        out_shape=[jax.ShapeDtypeStruct(shape, F32) for shape in shapes],
        in_specs=[VMEM],
        out_specs=[VMEM] * 6,
        name="unpack",
        compiler_params=room(6),
    )(sums)


def shift(value, axes, step):
    count = lax.axis_size(axes)
    pairs = [(i, i + step) for i in range(count) if 0 <= i + step < count]
    return lax.ppermute(value, axes, pairs)


def per_device(
    signal,
    kernel_front,
    mixing_front,
    offset_front,
    kernel_back,
    mixing_back,
    offset_back,
    upstream,
):
    pack = lambda part: jnp.concatenate([part[:, :PACK], part[:, PACK:]], axis=2)
    join = lambda *parts: jnp.concatenate(parts, axis=1)
    low = shift(join(signal, pack(upstream[:, :, 64:])), TICK, 1)
    high = shift(join(signal, pack(upstream[:, :, :64])), TICK, -1)

    sig, *tables, own_up, own_down = call_prepare(
        signal,
        upstream,
        kernel_front.reshape(CHANNELS, 27),
        kernel_back.reshape(CHANNELS, 27),
        jnp.stack([mixing_front.T, mixing_back.T, mixing_back, mixing_front]),
        jnp.stack([offset_front, offset_back]),
    )
    strip_up, strip_down, sig, *tables = call_cut(low, high, own_up, own_down, sig, *tables)
    h_up, h_down = shift(strip_down, WIRE, 1), shift(strip_up, WIRE, -1)
    place = jnp.stack([lax.axis_index(TICK), lax.axis_index(WIRE)]).astype(jnp.int32)
    held = call_inner(place, low, high, upstream, sig, *tables)
    response, signal_grad, sums = call_border(place, h_up, h_down, *held, *tables)
    for group in REDUCTION_ORDER:
        sums = lax.psum(sums, group)
    factor = 1.0 / math.sqrt(WIRES * lax.axis_size(WIRE) * TICKS * lax.axis_size(TICK))
    front_taps, front_square, front_line, back_taps, back_square, back_line = call_unpack(
        sums, factor
    )
    return (
        response,
        signal_grad,
        front_taps.transpose(2, 1, 0),
        front_square,
        front_line.reshape(CHANNELS),
        back_taps.transpose(2, 1, 0),
        back_square,
        back_line.reshape(CHANNELS),
    )


def solution(mesh):
    fine = Mesh(mesh.devices.reshape(8, 4, 2, 2, 4), TICK + WIRE)
    block = P(None, WIRE, TICK)
    in_specs = (block, P(), P(), P(), P(), P(), P(), block)
    out_specs = (block, block, P(), P(), P(), P(), P(), P())
    return jax.shard_map(
        per_device, mesh=fine, in_specs=in_specs, out_specs=out_specs, check_vma=False
    )
```

```python
import functools
import math

import jax
import jax.numpy as jnp
from jax import lax
from jax.experimental import pallas as pl
from jax.experimental.pallas import tpu as pltpu
from jax.sharding import Mesh, PartitionSpec as P

TICK = ("y", "z_hi", "core")
WIRE = ("z_lo", "x")
REDUCTION_ORDER = ("core", "x", ("z_hi", "z_lo"), "y")

CHANNELS, WIRES, TICKS = 16, 64, 128
STEP = 8
BLOCKS = TICKS // STEP
MARGIN = 4
OWN = 12
DEEP = 88
PACK = WIRES // 2
TILE = 128
F32, BF16 = jnp.float32, jnp.bfloat16


def lanes(shape):
    return lax.broadcasted_iota(jnp.int32, shape, len(shape) - 1)


def turn(tile, shift):
    return pltpu.roll(tile, shift, 1) if shift else tile


def exchange(tiles):
    lane = lanes(tiles[0].shape)
    tiles = [turn(tile, STEP * c) for c, tile in enumerate(tiles)]
    tiles = [tiles[-k % 16] for k in range(16)]
    for bit in range(4):
        upper = (lane & (STEP << bit)) != 0
        tiles = [jnp.where(upper, tiles[k - (1 << bit)], tiles[k]) for k in range(16)]
    return [turn(tile, (TILE - STEP * a) % TILE) for a, tile in enumerate(tiles)]


def tap(row, column, flip):
    return (2 - row) * 9 + 8 - column if flip else row * 9 + column


def convolve(source, target, kernel, flip, planes, first, last):
    def group(index, _):
        base = OWN + jnp.minimum(first + 8 * index, last - 8)
        weights = [[kernel[tap(i, j, flip)] for j in range(9)] for i in range(3)]
        sums = {}
        for at in range(planes + 8):
            rows = [source[at, pl.ds(base + i - 1, 8), :] for i in range(3)]
            for j in range(9):
                plane = at - j
                if not 0 <= plane < planes:
                    continue
                value = weights[0][j] * rows[0] + weights[1][j] * rows[1] + weights[2][j] * rows[2]
                sums[plane] = sums[plane] + value if j else value
                if j == 8:
                    target[plane, pl.ds(base, 8), :] = sums.pop(plane)
        return 0

    lax.fori_loop(0, (last - first + 7) // 8, group, 0)


def correlate(upward, ahead, source, start, lines, place):
    def group(index, carry):
        base = OWN + 8 * index
        sums = list(carry)
        ups = {}
        for at in range(BLOCKS + 8):
            if at < BLOCKS:
                ups[at] = upward[ahead + at, pl.ds(base, 8), :]
            rows = [source[start + at, pl.ds(base + i - 1, 8), :] for i in range(3)]
            for j in range(9):
                if 0 <= at - j < BLOCKS:
                    for i in range(3):
                        sums[9 * i + j] = sums[9 * i + j] + ups[at - j] * rows[i]
        return tuple(sums)

    zero = tuple(jnp.zeros((8, TILE), F32) for _ in range(27))
    sums = lax.fori_loop(0, WIRES // 8, group, zero)
    for k in range(27):
        lines[place + k : place + k + 1, :] = jnp.sum(sums[k], axis=0, keepdims=True)


def split(value):
    high = value.astype(BF16)
    return high, (value - high.astype(F32)).astype(BF16)


def mix(value, matrix):
    both = jnp.dot(jnp.concatenate(split(value), axis=1), matrix, preferred_element_type=F32)
    return both[:, :TILE] + both[:, TILE:]


def outer(left, right):
    lh, ll = split(left)
    rh, rl = split(right)
    return lax.dot_general(
        jnp.concatenate([lh, lh, ll], axis=0),
        jnp.concatenate([rh, rl, rh], axis=0),
        (((0,), (0,)), ((), ())),
        preferred_element_type=F32,
    )


def exact(left, right, contract):
    return lax.dot_general(
        left,
        right,
        (contract, ((), ())),
        precision=lax.Precision.HIGHEST,
        preferred_element_type=F32,
    )


PLANES = dict(
    sig=48, ups=32, fields_f=40, act=40, slope=40, fields_b=32, grads_b=32, u_back=32, result=32,
    grads_f=24, u_front=24, back_out=16,
)

AHEAD = ("sig", "fields_f", "act", "slope")
BEHIND = tuple(name for name in PLANES if name not in AHEAD)


def load(source, row):
    return exchange([source[c, pl.ds(row, 8), :] for c in range(CHANNELS)])


class Stages:
    def __init__(self, held, halves, biases, place):
        self.__dict__.update(held)
        self.halves, self.biases, self.place = halves, biases, place

    def front(self, at, count, wire, wires, margin):
        rows = pl.ds(OWN + wire, wires)
        value = self.fields_f[pl.ds(at, count), rows, :].reshape(count * wires, TILE)
        value = mix(value, self.halves[0]) + self.biases[0:1, :]
        order = lax.broadcasted_iota(jnp.int32, (count, wires, TILE), 0)
        tick_at, wire_at = self.place[0], self.place[1]
        plane = at + order
        inside = jnp.logical_and(
            jnp.logical_or(plane >= 12, tick_at > 0), jnp.logical_or(plane < 28, tick_at < 63)
        )
        if margin:
            line = wire + lax.broadcasted_iota(jnp.int32, (count, wires, TILE), 1)
            inside = jnp.logical_and(
                inside,
                jnp.logical_and(
                    jnp.logical_or(line >= 0, wire_at > 0),
                    jnp.logical_or(line < WIRES, wire_at < 7),
                ),
            )
        sigmoid = 1.0 / (1.0 + jnp.exp(-value))
        act = (value * sigmoid).reshape(count, wires, TILE)
        slope = (sigmoid * (1.0 + value * (1.0 - sigmoid))).reshape(count, wires, TILE)
        self.act[pl.ds(at, count), rows, :] = jnp.where(inside, act, 0.0)
        self.slope[pl.ds(at, count), rows, :] = jnp.where(inside, slope, 0.0)

    def back(self, at, count, wire, wires):
        rows = pl.ds(OWN + wire, wires)
        here = lambda planes: planes[pl.ds(at, count), rows, :].reshape(count * wires, TILE)
        value = mix(here(self.fields_b), self.halves[1]) + self.biases[1:2, :]
        sigmoid = 1.0 / (1.0 + jnp.exp(-value))
        grad = here(self.ups) * (sigmoid * (1.0 + value * (1.0 - sigmoid)))
        under = mix(grad, self.halves[2])
        for planes, field in (
            (self.result, value * sigmoid), (self.grads_b, grad), (self.u_back, under)
        ):
            planes[pl.ds(at, count), rows, :] = field.reshape(count, wires, TILE)

    def under_front(self, fields, at, count, wire, wires):
        rows = pl.ds(OWN + wire, wires)
        grad = fields[pl.ds(at, count), rows, :] * self.slope[pl.ds(at + 8, count), rows, :]
        under = mix(grad.reshape(count * wires, TILE), self.halves[3])
        self.grads_f[pl.ds(at, count), rows, :] = grad
        self.u_front[pl.ds(at, count), rows, :] = under.reshape(count, wires, TILE)


def loop(count, step, unroll):
    def one(index, _):
        step(index)
        return 0

    lax.fori_loop(0, count, one, 0, unroll=unroll)


def prepare(s_own, u_own, taps_front, taps_back, mixings, offsets, *rest):
    sig, kernel_front, kernel_back, halves, biases, own_up, own_down = rest
    for strip, rows in ((own_up, pl.ds(0, MARGIN)), (own_down, pl.ds(WIRES - MARGIN, MARGIN))):
        strip[:, :MARGIN, :] = s_own[:, rows, :]
        strip[:, MARGIN:, :] = u_own[:, rows, :]
    spread = (lanes((CHANNELS, TILE)) // STEP) == lax.broadcasted_iota(
        jnp.int32, (CHANNELS, TILE), 0
    )
    spread = jnp.where(spread, 1.0, 0.0)
    for kernel, raw in ((kernel_front, taps_front), (kernel_back, taps_back)):
        wide = exact(raw[...], spread, ((0,), (0,)))
        for k in range(27):
            kernel[k] = jnp.broadcast_to(wide[k : k + 1, :], (8, TILE))
    biases[...] = exact(offsets[...], spread, ((1,), (0,)))
    same = (lanes((TILE, TILE)) % STEP) == (
        lax.broadcasted_iota(jnp.int32, (TILE, TILE), 0) % STEP
    )
    for k in range(4):
        wide = exact(exact(spread, mixings[k], ((0,), (0,))), spread, ((1,), (0,)))
        upper, lower = split(jnp.where(same, wide, 0.0))
        halves[k, 0:TILE, 0:TILE] = upper
        halves[k, 0:TILE, TILE:] = lower
        halves[k, TILE:, 0:TILE] = upper
        halves[k, TILE:, TILE:] = jnp.zeros((TILE, TILE), BF16)

    def fill(group):
        row = pl.multiple_of(8 * group, 8)
        for a, tile in enumerate(load(s_own, row)):
            sig[BLOCKS + a, pl.ds(OWN + row, 8), :] = tile

    loop(WIRES // 8, fill, 1)


def cut(s_low, s_high, u_low, u_high, own_up, own_down, *rest):
    strip_up, strip_down = rest[8:10]
    slabs, arrived = rest[-2:]
    copies = []
    signals, upstreams = (s_low, s_high), (u_low, u_high)
    for k, (row, sources) in enumerate(
        ((0, signals), (0, upstreams), (WIRES - 8, signals), (PACK - 8, upstreams))
    ):
        for side, source in enumerate(sources):
            at = 2 * k + side
            copies.append(
                pltpu.make_async_copy(
                    source.at[:, pl.ds(row, 8), :], slabs.at[at], arrived.at[at]
                )
            )
    for copy in copies:
        copy.start()
    for copy in copies:
        copy.wait()
    for strip, own, first, rows in (
        (strip_up, own_up, 0, slice(0, MARGIN)),
        (strip_down, own_down, 4, slice(MARGIN, 8)),
    ):
        strip[:, 0:8, :] = own[...]
        for k in range(4):
            strip[:, 8 + MARGIN * k : 8 + MARGIN * (k + 1), :] = slabs[first + k, :, rows, :]


def first(place, low, high, *rest):
    kernel_front, kernel_back, halves, biases = rest[1:5]
    do = Stages(dict(zip(AHEAD, rest[5:])), halves, biases, place)

    def fill(group):
        row = pl.multiple_of(8 * group, 8)
        for source, start in ((low, 0), (high, 2 * BLOCKS)):
            for a, tile in enumerate(load(source, row)):
                do.sig[start + a, pl.ds(OWN + row, 8), :] = tile

    loop(WIRES // 8, fill, 1)
    convolve(do.sig, do.fields_f, kernel_front, False, 40, 1, 63)
    loop(20, lambda k: do.front(2 * k, 2, 0, WIRES, False), 10)


def inner(place, low, high, u_own, act, slope, *rest):
    kernel_front, kernel_back, halves, biases = rest[:4]
    held = dict(zip(BEHIND, rest[4:]), act=act, slope=slope)
    fields_d = rest[-1]
    do = Stages(held, halves, biases, place)

    def fill(group):
        row = pl.multiple_of(8 * group, 8)
        for a, tile in enumerate(load(u_own, row)):
            do.ups[BLOCKS // 2 + a, pl.ds(OWN + row, 8), :] = tile

    loop(WIRES // 8, fill, 2)

    def fill_packed(group):
        row = pl.multiple_of(8 * group, 8)
        for source, start in ((low, 0), (high, BLOCKS // 2 + BLOCKS)):
            for a, tile in enumerate(load(source, row)):
                second, plane = divmod(a, BLOCKS // 2)
                do.ups[start + plane, pl.ds(OWN + row + second * PACK, 8), :] = tile

    loop(PACK // 8, fill_packed, 1)
    convolve(do.act, do.fields_b, kernel_back, False, 32, 2, 62)
    loop(16, lambda k: do.back(2 * k, 2, 0, WIRES), 8)
    convolve(do.u_back, fields_d, kernel_back, True, 24, 3, 61)
    loop(12, lambda k: do.under_front(fields_d, 2 * k, 2, 0, WIRES), 6)
    convolve(do.u_front, do.back_out, kernel_front, True, 16, 4, 60)


def border(place, h_up, h_down, *rest):
    many = len(PLANES) + 4
    response, signal_grad, sums = rest[many : many + 3]
    held = dict(zip(PLANES, rest[many + 3 :]))
    kernel_front, kernel_back, halves, biases = rest[len(PLANES) : many]
    fields_d, lines = rest[many + 3 + len(PLANES) :]
    do = Stages(held, halves, biases, place)
    sig, ups = do.sig, do.ups

    for second, base, strip in ((1, OWN - MARGIN, h_up), (0, OWN + WIRES, h_down)):
        pairs = [load(strip, 8 * k) for k in range(3)]
        for a in range(BLOCKS):
            sig[BLOCKS + a, base : base + MARGIN, :] = pairs[0][a][:MARGIN]
            ups[BLOCKS // 2 + a, base : base + MARGIN, :] = pairs[0][a][MARGIN:]
            sig[a, base : base + MARGIN, :] = pairs[1][a][:MARGIN]
            sig[2 * BLOCKS + a, base : base + MARGIN, :] = pairs[1][a][MARGIN:]
            plane = a - second * (BLOCKS // 2)
            if 0 <= plane < BLOCKS // 2:
                ups[plane, base : base + MARGIN, :] = pairs[2][a][:MARGIN]
                ups[BLOCKS // 2 + BLOCKS + plane, base : base + MARGIN, :] = pairs[2][a][MARGIN:]

    for start in (-3, 59):
        convolve(sig, do.fields_f, kernel_front, False, 40, start, start + 8)
    for start in (-3, 59):
        do.front(0, 40, start, 8, True)
    for start in (-2, 58):
        convolve(do.act, do.fields_b, kernel_back, False, 32, start, start + 8)
    for start in (-2, 58):
        do.back(0, 32, start, 8)
    for start in (-1, 57):
        convolve(do.u_back, fields_d, kernel_back, True, 24, start, start + 8)
    for start in (-1, 57):
        do.under_front(fields_d, 0, 24, start, 8)
    for start in (0, 56):
        convolve(do.u_front, do.back_out, kernel_front, True, 16, start, start + 8)

    lines[...] = jnp.zeros_like(lines)
    same = (lanes((TILE, TILE)) % STEP) == (
        lax.broadcasted_iota(jnp.int32, (TILE, TILE), 0) % STEP
    )

    def give(group):
        row = pl.multiple_of(8 * group, 8)
        for source, start, target in ((do.result, 8, response), (do.back_out, 0, signal_grad)):
            tiles = [source[start + a, pl.ds(OWN + row, 8), :] for a in range(BLOCKS)]
            for c, tile in enumerate(exchange(tiles)):
                target[c, pl.ds(row, 8), :] = tile

    loop(WIRES // 8, give, 1)

    def tally(grads, ahead, fields, start, square_at, line_at):
        own = pl.ds(OWN, WIRES)

        def some(pair, carry):
            square, line = carry
            grad = grads[pl.ds(ahead + 2 * pair, 2), own, :].reshape(2 * WIRES, TILE)
            field = fields[pl.ds(start + 2 * pair, 2), own, :].reshape(2 * WIRES, TILE)
            line = line + jnp.sum(grad.reshape(2 * WIRES // 8, 8, TILE), axis=0)
            return square + outer(grad, field), line

        square, line = lax.fori_loop(
            0,
            BLOCKS // 2,
            some,
            (jnp.zeros((TILE, TILE), F32), jnp.zeros((8, TILE), F32)),
            unroll=8,
        )
        square = jnp.where(same, square, 0.0).reshape(CHANNELS, STEP, TILE)
        lines[square_at : square_at + CHANNELS, :] = jnp.sum(square, axis=1)
        lines[line_at : line_at + 1, :] = jnp.sum(line, axis=0, keepdims=True)

    tally(do.grads_b, 8, do.fields_b, 8, 64, 27)
    tally(do.grads_f, 4, do.fields_f, 12, 80, 59)
    correlate(do.u_back, 8, do.act, 8, lines, 0)
    correlate(do.u_front, 4, sig, 12, lines, 32)

    found = lines[...]
    for step in (1, 2, 4):
        found = found + pltpu.roll(found, TILE - step, 1)
    row = lax.broadcasted_iota(jnp.int32, (8, TILE), 0)
    sums[12:16, :] = jnp.zeros((4, TILE), F32)
    for k in range(12):
        turned = pltpu.roll(found[8 * k : 8 * k + 8], 0, 1, stride=1, stride_axis=0)
        sums[k : k + 1, :] = jnp.sum(
            jnp.where(lanes((8, TILE)) % STEP == row, turned, 0.0), axis=0, keepdims=True
        )


VMEM = pl.BlockSpec(memory_space=pltpu.VMEM)
SMEM = pl.BlockSpec(memory_space=pltpu.SMEM)


def room(mebibytes):
    return pltpu.CompilerParams(vmem_limit_bytes=mebibytes * 1024 * 1024)


HELD = [jax.ShapeDtypeStruct((count, DEEP, TILE), F32) for count in PLANES.values()]


FRONT = [jax.ShapeDtypeStruct((PLANES[name], DEEP, TILE), F32) for name in AHEAD]
BACK = [jax.ShapeDtypeStruct((PLANES[name], DEEP, TILE), F32) for name in BEHIND]
TABLES = [
    jax.ShapeDtypeStruct((27, 8, TILE), F32),
    jax.ShapeDtypeStruct((27, 8, TILE), F32),
    jax.ShapeDtypeStruct((4, 2 * TILE, 2 * TILE), BF16),
    jax.ShapeDtypeStruct((2, TILE), F32),
]


def call_prepare(*arrays):
    return pl.pallas_call(
        prepare,
        out_shape=HELD[:1] + TABLES + [jax.ShapeDtypeStruct((CHANNELS, 8, TICKS), F32)] * 2,
        in_specs=[VMEM] * len(arrays),
        out_specs=[VMEM] * 7,
        name="prepare",
        compiler_params=room(12),
    )(*arrays)


def call_cut(*arrays):
    strip = jax.ShapeDtypeStruct((CHANNELS, 24, TICKS), F32)
    return pl.pallas_call(
        cut,
        out_shape=[strip, strip] + FRONT + TABLES,
        in_specs=[pl.BlockSpec(memory_space=pl.ANY)] * 4 + [VMEM] * (len(arrays) - 4),
        out_specs=[VMEM] * 10,
        scratch_shapes=[
            pltpu.VMEM((8, CHANNELS, 8, TICKS), F32),
            pltpu.SemaphoreType.DMA((8,)),
        ],
        input_output_aliases={6 + k: 2 + k for k in range(8)},
        name="cut",
        compiler_params=room(24),
    )(*arrays)


def call_first(*arrays):
    return pl.pallas_call(
        first,
        out_shape=FRONT,
        in_specs=[SMEM] + [VMEM] * (len(arrays) - 1),
        out_specs=[VMEM] * 4,
        input_output_aliases={3: 0},
        name="first",
        compiler_params=room(24),
    )(*arrays)


def call_inner(*arrays):
    return pl.pallas_call(
        inner,
        out_shape=BACK,
        in_specs=[SMEM] + [VMEM] * (len(arrays) - 1),
        out_specs=[VMEM] * len(BACK),
        scratch_shapes=[pltpu.VMEM((24, DEEP, TILE), F32)],
        name="inner",
        compiler_params=room(24),
    )(*arrays)


def call_border(*arrays):
    field = jax.ShapeDtypeStruct((CHANNELS, WIRES, TICKS), F32)
    return pl.pallas_call(
        border,
        out_shape=[field, field, jax.ShapeDtypeStruct((16, TILE), F32)] + HELD,
        in_specs=[SMEM] + [VMEM] * (len(arrays) - 1),
        out_specs=[VMEM] * (3 + len(HELD)),
        scratch_shapes=[
            pltpu.VMEM((24, DEEP, TILE), F32),
            pltpu.VMEM((96, TILE), F32),
        ],
        input_output_aliases={3 + k: 3 + k for k in range(len(HELD))},
        name="border",
        compiler_params=room(24),
    )(*arrays)[:3]


def unpack(sums, front_taps, front_square, front_line, back_taps, back_square, back_line, factor):
    row = lax.broadcasted_iota(jnp.int32, (16, STEP, TILE), 1)
    wide = jnp.broadcast_to(sums[...][:, None, :], (16, STEP, TILE))
    wide = jnp.where(lanes(wide.shape) % STEP == row, wide, 0.0).reshape(16 * STEP, TILE)
    channel = lax.broadcasted_iota(jnp.int32, (TILE, CHANNELS), 0) // STEP
    pick = jnp.where(channel == lanes((TILE, CHANNELS)), 1.0, 0.0)
    rows = exact(wide, pick, ((1,), (0,))) * factor
    for taps, square, line, first, square_at, line_at in (
        (front_taps, front_square, front_line, 32, 80, 59),
        (back_taps, back_square, back_line, 0, 64, 27),
    ):
        for i in range(3):
            for j in range(9):
                at = first + 9 * i + j
                taps[j, i : i + 1, :] = rows[at : at + 1, :]
        square[...] = rows[square_at : square_at + CHANNELS, :]
        line[...] = rows[line_at : line_at + 1, :]


def call_unpack(sums, factor):
    shapes = [(9, 3, CHANNELS), (CHANNELS, CHANNELS), (1, CHANNELS)] * 2
    return pl.pallas_call(
        functools.partial(unpack, factor=factor),
        out_shape=[jax.ShapeDtypeStruct(shape, F32) for shape in shapes],
        in_specs=[VMEM],
        out_specs=[VMEM] * 6,
        name="unpack",
        compiler_params=room(6),
    )(sums)


def shift(value, axes, step):
    count = lax.axis_size(axes)
    pairs = [(i, i + step) for i in range(count) if 0 <= i + step < count]
    return lax.ppermute(value, axes, pairs)


def per_device(
    signal,
    kernel_front,
    mixing_front,
    offset_front,
    kernel_back,
    mixing_back,
    offset_back,
    upstream,
):
    pack = lambda part: jnp.concatenate([part[:, :PACK], part[:, PACK:]], axis=2)
    place = jnp.stack([lax.axis_index(TICK), lax.axis_index(WIRE)]).astype(jnp.int32)
    s_low, s_high = shift(signal, TICK, 1), shift(signal, TICK, -1)
    u_low = shift(pack(upstream[:, :, 64:]), TICK, 1)
    u_high = shift(pack(upstream[:, :, :64]), TICK, -1)
    sig, *tables, own_up, own_down = call_prepare(
        signal,
        upstream,
        kernel_front.reshape(CHANNELS, 27),
        kernel_back.reshape(CHANNELS, 27),
        jnp.stack([mixing_front.T, mixing_back.T, mixing_back, mixing_front]),
        jnp.stack([offset_front, offset_back]),
    )
    ahead = call_first(place, s_low, s_high, sig, *tables)
    strip_up, strip_down, *rest = call_cut(
        s_low, s_high, u_low, u_high, own_up, own_down, *ahead, *tables
    )
    ahead, tables = rest[:4], rest[4:]
    h_up, h_down = shift(strip_down, WIRE, 1), shift(strip_up, WIRE, -1)
    behind = call_inner(place, u_low, u_high, upstream, *ahead[2:], *tables)
    held = {**dict(zip(AHEAD, ahead)), **dict(zip(BEHIND, behind))}
    response, signal_grad, sums = call_border(
        place, h_up, h_down, *(held[name] for name in PLANES), *tables
    )
    for group in REDUCTION_ORDER:
        sums = lax.psum(sums, group)
    factor = 1.0 / math.sqrt(WIRES * lax.axis_size(WIRE) * TICKS * lax.axis_size(TICK))
    front_taps, front_square, front_line, back_taps, back_square, back_line = call_unpack(
        sums, factor
    )
    return (
        response,
        signal_grad,
        front_taps.transpose(2, 1, 0),
        front_square,
        front_line.reshape(CHANNELS),
        back_taps.transpose(2, 1, 0),
        back_square,
        back_line.reshape(CHANNELS),
    )


def solution(mesh):
    fine = Mesh(mesh.devices.reshape(8, 4, 2, 2, 4), TICK + WIRE)
    block = P(None, WIRE, TICK)
    in_specs = (block, P(), P(), P(), P(), P(), P(), block)
    out_specs = (block, block, P(), P(), P(), P(), P(), P())
    return jax.shard_map(
        per_device, mesh=fine, in_specs=in_specs, out_specs=out_specs, check_vma=False
    )
```

```python
import functools
import math

import jax
import jax.numpy as jnp
from jax import lax
from jax.experimental import pallas as pl
from jax.experimental.pallas import tpu as pltpu
from jax.sharding import Mesh, PartitionSpec as P

TICK = ("y", "z_hi", "core")
WIRE = ("z_lo", "x")
REDUCTION_ORDER = ("core", "x", ("z_hi", "z_lo"), "y")

CHANNELS, WIRES, TICKS = 16, 64, 128
STEP = 8
BLOCKS = TICKS // STEP
MARGIN = 4
OWN = 12
DEEP = 88
PACK = WIRES // 2
TILE = 128
F32, BF16 = jnp.float32, jnp.bfloat16


def lanes(shape):
    return lax.broadcasted_iota(jnp.int32, shape, len(shape) - 1)


def turn(tile, shift):
    return pltpu.roll(tile, shift, 1) if shift else tile


def exchange(tiles):
    lane = lanes(tiles[0].shape)
    tiles = [turn(tile, STEP * c) for c, tile in enumerate(tiles)]
    tiles = [tiles[-k % 16] for k in range(16)]
    for bit in range(4):
        upper = (lane & (STEP << bit)) != 0
        tiles = [jnp.where(upper, tiles[k - (1 << bit)], tiles[k]) for k in range(16)]
    return [turn(tile, (TILE - STEP * a) % TILE) for a, tile in enumerate(tiles)]


def tap(row, column, flip):
    return (2 - row) * 9 + 8 - column if flip else row * 9 + column


def convolve(source, target, kernel, flip, planes, first, last):
    def group(index, _):
        base = OWN + jnp.minimum(first + 8 * index, last - 8)
        weights = [[kernel[tap(i, j, flip)] for j in range(9)] for i in range(3)]
        sums = {}
        for at in range(planes + 8):
            rows = [source[at, pl.ds(base + i - 1, 8), :] for i in range(3)]
            for j in range(9):
                plane = at - j
                if not 0 <= plane < planes:
                    continue
                value = weights[0][j] * rows[0] + weights[1][j] * rows[1] + weights[2][j] * rows[2]
                sums[plane] = sums[plane] + value if j else value
                if j == 8:
                    target[plane, pl.ds(base, 8), :] = sums.pop(plane)
        return 0

    lax.fori_loop(0, (last - first + 7) // 8, group, 0)


def correlate(upward, ahead, source, start, lines, place):
    def group(index, carry):
        base = OWN + 8 * index
        sums = list(carry)
        ups = {}
        for at in range(BLOCKS + 8):
            if at < BLOCKS:
                ups[at] = upward[ahead + at, pl.ds(base, 8), :]
            rows = [source[start + at, pl.ds(base + i - 1, 8), :] for i in range(3)]
            for j in range(9):
                if 0 <= at - j < BLOCKS:
                    for i in range(3):
                        sums[9 * i + j] = sums[9 * i + j] + ups[at - j] * rows[i]
        return tuple(sums)

    zero = tuple(jnp.zeros((8, TILE), F32) for _ in range(27))
    sums = lax.fori_loop(0, WIRES // 8, group, zero)
    for k in range(27):
        lines[place + k : place + k + 1, :] = jnp.sum(sums[k], axis=0, keepdims=True)


def split(value):
    high = value.astype(BF16)
    return high, (value - high.astype(F32)).astype(BF16)


def mix(value, matrix):
    both = jnp.dot(jnp.concatenate(split(value), axis=1), matrix, preferred_element_type=F32)
    return both[:, :TILE] + both[:, TILE:]


def outer(left, right):
    lh, ll = split(left)
    rh, rl = split(right)
    return lax.dot_general(
        jnp.concatenate([lh, lh, ll], axis=0),
        jnp.concatenate([rh, rl, rh], axis=0),
        (((0,), (0,)), ((), ())),
        preferred_element_type=F32,
    )


def exact(left, right, contract):
    return lax.dot_general(
        left,
        right,
        (contract, ((), ())),
        precision=lax.Precision.HIGHEST,
        preferred_element_type=F32,
    )


PLANES = dict(
    sig=48, ups=32, fields_f=40, act=40, slope=40, fields_b=32, grads_b=32, u_back=32, result=32,
    grads_f=24, u_front=24, back_out=16,
)

AHEAD = ("sig", "fields_f", "act", "slope")
BEHIND = tuple(name for name in PLANES if name not in AHEAD)


def load(source, row):
    return exchange([source[c, pl.ds(row, 8), :] for c in range(CHANNELS)])


class Stages:
    def __init__(self, held, halves, biases, place):
        self.__dict__.update(held)
        self.halves, self.biases, self.place = halves, biases, place

    def front(self, at, count, wire, wires, margin):
        rows = pl.ds(OWN + wire, wires)
        value = self.fields_f[pl.ds(at, count), rows, :].reshape(count * wires, TILE)
        value = mix(value, self.halves[0]) + self.biases[0:1, :]
        order = lax.broadcasted_iota(jnp.int32, (count, wires, TILE), 0)
        tick_at, wire_at = self.place[0], self.place[1]
        plane = at + order
        inside = jnp.logical_and(
            jnp.logical_or(plane >= 12, tick_at > 0), jnp.logical_or(plane < 28, tick_at < 63)
        )
        if margin:
            line = wire + lax.broadcasted_iota(jnp.int32, (count, wires, TILE), 1)
            inside = jnp.logical_and(
                inside,
                jnp.logical_and(
                    jnp.logical_or(line >= 0, wire_at > 0),
                    jnp.logical_or(line < WIRES, wire_at < 7),
                ),
            )
        sigmoid = 1.0 / (1.0 + jnp.exp(-value))
        act = (value * sigmoid).reshape(count, wires, TILE)
        slope = (sigmoid * (1.0 + value * (1.0 - sigmoid))).reshape(count, wires, TILE)
        self.act[pl.ds(at, count), rows, :] = jnp.where(inside, act, 0.0)
        self.slope[pl.ds(at, count), rows, :] = jnp.where(inside, slope, 0.0)

    def back(self, at, count, wire, wires):
        rows = pl.ds(OWN + wire, wires)
        here = lambda planes: planes[pl.ds(at, count), rows, :].reshape(count * wires, TILE)
        value = mix(here(self.fields_b), self.halves[1]) + self.biases[1:2, :]
        sigmoid = 1.0 / (1.0 + jnp.exp(-value))
        grad = here(self.ups) * (sigmoid * (1.0 + value * (1.0 - sigmoid)))
        under = mix(grad, self.halves[2])
        for planes, field in (
            (self.result, value * sigmoid), (self.grads_b, grad), (self.u_back, under)
        ):
            planes[pl.ds(at, count), rows, :] = field.reshape(count, wires, TILE)

    def under_front(self, fields, at, count, wire, wires):
        rows = pl.ds(OWN + wire, wires)
        grad = fields[pl.ds(at, count), rows, :] * self.slope[pl.ds(at + 8, count), rows, :]
        under = mix(grad.reshape(count * wires, TILE), self.halves[3])
        self.grads_f[pl.ds(at, count), rows, :] = grad
        self.u_front[pl.ds(at, count), rows, :] = under.reshape(count, wires, TILE)


def loop(count, step, unroll):
    def one(index, _):
        step(index)
        return 0

    lax.fori_loop(0, count, one, 0, unroll=unroll)


def prepare(s_own, u_own, taps_front, taps_back, mixings, offsets, *rest):
    sig, kernel_front, kernel_back, halves, biases, own_up, own_down = rest
    for strip, rows in ((own_up, pl.ds(0, MARGIN)), (own_down, pl.ds(WIRES - MARGIN, MARGIN))):
        strip[:, :MARGIN, :] = s_own[:, rows, :]
        strip[:, MARGIN:, :] = u_own[:, rows, :]
    spread = (lanes((CHANNELS, TILE)) // STEP) == lax.broadcasted_iota(
        jnp.int32, (CHANNELS, TILE), 0
    )
    spread = jnp.where(spread, 1.0, 0.0)
    for kernel, raw in ((kernel_front, taps_front), (kernel_back, taps_back)):
        wide = exact(raw[...], spread, ((0,), (0,)))
        for k in range(27):
            kernel[k] = jnp.broadcast_to(wide[k : k + 1, :], (8, TILE))
    biases[...] = exact(offsets[...], spread, ((1,), (0,)))
    same = (lanes((TILE, TILE)) % STEP) == (
        lax.broadcasted_iota(jnp.int32, (TILE, TILE), 0) % STEP
    )
    for k in range(4):
        wide = exact(exact(spread, mixings[k], ((0,), (0,))), spread, ((1,), (0,)))
        upper, lower = split(jnp.where(same, wide, 0.0))
        halves[k, 0:TILE, 0:TILE] = upper
        halves[k, 0:TILE, TILE:] = lower
        halves[k, TILE:, 0:TILE] = upper
        halves[k, TILE:, TILE:] = jnp.zeros((TILE, TILE), BF16)

    def fill(group):
        row = pl.multiple_of(8 * group, 8)
        for a, tile in enumerate(load(s_own, row)):
            sig[BLOCKS + a, pl.ds(OWN + row, 8), :] = tile

    loop(WIRES // 8, fill, 1)


def cut(s_low, s_high, u_low, u_high, own_up, own_down, *rest):
    strip_up, strip_down = rest[8:10]
    slabs, arrived = rest[-2:]
    copies = []
    signals, upstreams = (s_low, s_high), (u_low, u_high)
    for k, (row, sources) in enumerate(
        ((0, signals), (0, upstreams), (WIRES - 8, signals), (PACK - 8, upstreams))
    ):
        for side, source in enumerate(sources):
            at = 2 * k + side
            copies.append(
                pltpu.make_async_copy(
                    source.at[:, pl.ds(row, 8), :], slabs.at[at], arrived.at[at]
                )
            )
    for copy in copies:
        copy.start()
    for copy in copies:
        copy.wait()
    for strip, own, first, rows in (
        (strip_up, own_up, 0, slice(0, MARGIN)),
        (strip_down, own_down, 4, slice(MARGIN, 8)),
    ):
        strip[:, 0:8, :] = own[...]
        for k in range(4):
            strip[:, 8 + MARGIN * k : 8 + MARGIN * (k + 1), :] = slabs[first + k, :, rows, :]


def first(place, low, high, *rest):
    kernel_front, kernel_back, halves, biases = rest[1:5]
    do = Stages(dict(zip(AHEAD, rest[5:])), halves, biases, place)

    def fill(group):
        for row in (pl.multiple_of(16 * group, 8), pl.multiple_of(16 * group + 8, 8)):
            for source, start in ((low, 0), (high, 2 * BLOCKS)):
                for a, tile in enumerate(load(source, row)):
                    do.sig[start + a, pl.ds(OWN + row, 8), :] = tile

    loop(WIRES // 16, fill, 1)
    convolve(do.sig, do.fields_f, kernel_front, False, 40, 1, 63)
    loop(20, lambda k: do.front(2 * k, 2, 0, WIRES, False), 10)


def inner(place, low, high, u_own, act, slope, *rest):
    kernel_front, kernel_back, halves, biases = rest[:4]
    held = dict(zip(BEHIND, rest[4:]), act=act, slope=slope)
    fields_d = rest[-1]
    do = Stages(held, halves, biases, place)

    def fill(group):
        for row in (pl.multiple_of(16 * group, 8), pl.multiple_of(16 * group + 8, 8)):
            for a, tile in enumerate(load(u_own, row)):
                do.ups[BLOCKS // 2 + a, pl.ds(OWN + row, 8), :] = tile
        row = pl.multiple_of(8 * group, 8)
        for source, start in ((low, 0), (high, BLOCKS // 2 + BLOCKS)):
            for a, tile in enumerate(load(source, row)):
                second, plane = divmod(a, BLOCKS // 2)
                do.ups[start + plane, pl.ds(OWN + row + second * PACK, 8), :] = tile

    loop(PACK // 8, fill, 1)
    convolve(do.act, do.fields_b, kernel_back, False, 32, 2, 62)
    loop(16, lambda k: do.back(2 * k, 2, 0, WIRES), 8)
    convolve(do.u_back, fields_d, kernel_back, True, 24, 3, 61)
    loop(12, lambda k: do.under_front(fields_d, 2 * k, 2, 0, WIRES), 6)
    convolve(do.u_front, do.back_out, kernel_front, True, 16, 4, 60)


def border(place, h_up, h_down, *rest):
    many = len(PLANES) + 4
    response, signal_grad, sums = rest[many : many + 3]
    held = dict(zip(PLANES, rest[many + 3 :]))
    kernel_front, kernel_back, halves, biases = rest[len(PLANES) : many]
    fields_d, lines = rest[many + 3 + len(PLANES) :]
    do = Stages(held, halves, biases, place)
    sig, ups = do.sig, do.ups

    for second, base, strip in ((1, OWN - MARGIN, h_up), (0, OWN + WIRES, h_down)):
        pairs = [load(strip, 8 * k) for k in range(3)]
        for a in range(BLOCKS):
            sig[BLOCKS + a, base : base + MARGIN, :] = pairs[0][a][:MARGIN]
            ups[BLOCKS // 2 + a, base : base + MARGIN, :] = pairs[0][a][MARGIN:]
            sig[a, base : base + MARGIN, :] = pairs[1][a][:MARGIN]
            sig[2 * BLOCKS + a, base : base + MARGIN, :] = pairs[1][a][MARGIN:]
            plane = a - second * (BLOCKS // 2)
            if 0 <= plane < BLOCKS // 2:
                ups[plane, base : base + MARGIN, :] = pairs[2][a][:MARGIN]
                ups[BLOCKS // 2 + BLOCKS + plane, base : base + MARGIN, :] = pairs[2][a][MARGIN:]

    for start in (-3, 59):
        convolve(sig, do.fields_f, kernel_front, False, 40, start, start + 8)
    for start in (-3, 59):
        do.front(0, 40, start, 8, True)
    for start in (-2, 58):
        convolve(do.act, do.fields_b, kernel_back, False, 32, start, start + 8)
    for start in (-2, 58):
        do.back(0, 32, start, 8)
    for start in (-1, 57):
        convolve(do.u_back, fields_d, kernel_back, True, 24, start, start + 8)
    for start in (-1, 57):
        do.under_front(fields_d, 0, 24, start, 8)
    for start in (0, 56):
        convolve(do.u_front, do.back_out, kernel_front, True, 16, start, start + 8)

    lines[...] = jnp.zeros_like(lines)
    same = (lanes((TILE, TILE)) % STEP) == (
        lax.broadcasted_iota(jnp.int32, (TILE, TILE), 0) % STEP
    )

    def give(group):
        row = pl.multiple_of(8 * group, 8)
        for source, start, target in ((do.result, 8, response), (do.back_out, 0, signal_grad)):
            tiles = [source[start + a, pl.ds(OWN + row, 8), :] for a in range(BLOCKS)]
            for c, tile in enumerate(exchange(tiles)):
                target[c, pl.ds(row, 8), :] = tile

    loop(WIRES // 8, give, 1)

    def tally(grads, ahead, fields, start, square_at, line_at):
        own = pl.ds(OWN, WIRES)

        def some(pair, carry):
            square, line = carry
            grad = grads[pl.ds(ahead + 2 * pair, 2), own, :].reshape(2 * WIRES, TILE)
            field = fields[pl.ds(start + 2 * pair, 2), own, :].reshape(2 * WIRES, TILE)
            line = line + jnp.sum(grad.reshape(2 * WIRES // 8, 8, TILE), axis=0)
            return square + outer(grad, field), line

        square, line = lax.fori_loop(
            0,
            BLOCKS // 2,
            some,
            (jnp.zeros((TILE, TILE), F32), jnp.zeros((8, TILE), F32)),
            unroll=8,
        )
        square = jnp.where(same, square, 0.0).reshape(CHANNELS, STEP, TILE)
        lines[square_at : square_at + CHANNELS, :] = jnp.sum(square, axis=1)
        lines[line_at : line_at + 1, :] = jnp.sum(line, axis=0, keepdims=True)

    tally(do.grads_b, 8, do.fields_b, 8, 64, 27)
    tally(do.grads_f, 4, do.fields_f, 12, 80, 59)
    correlate(do.u_back, 8, do.act, 8, lines, 0)
    correlate(do.u_front, 4, sig, 12, lines, 32)

    found = lines[...]
    for step in (1, 2, 4):
        found = found + pltpu.roll(found, TILE - step, 1)
    row = lax.broadcasted_iota(jnp.int32, (8, TILE), 0)
    sums[12:16, :] = jnp.zeros((4, TILE), F32)
    for k in range(12):
        turned = pltpu.roll(found[8 * k : 8 * k + 8], 0, 1, stride=1, stride_axis=0)
        sums[k : k + 1, :] = jnp.sum(
            jnp.where(lanes((8, TILE)) % STEP == row, turned, 0.0), axis=0, keepdims=True
        )


VMEM = pl.BlockSpec(memory_space=pltpu.VMEM)
SMEM = pl.BlockSpec(memory_space=pltpu.SMEM)


def room(mebibytes):
    return pltpu.CompilerParams(vmem_limit_bytes=mebibytes * 1024 * 1024)


HELD = [jax.ShapeDtypeStruct((count, DEEP, TILE), F32) for count in PLANES.values()]


FRONT = [jax.ShapeDtypeStruct((PLANES[name], DEEP, TILE), F32) for name in AHEAD]
BACK = [jax.ShapeDtypeStruct((PLANES[name], DEEP, TILE), F32) for name in BEHIND]
TABLES = [
    jax.ShapeDtypeStruct((27, 8, TILE), F32),
    jax.ShapeDtypeStruct((27, 8, TILE), F32),
    jax.ShapeDtypeStruct((4, 2 * TILE, 2 * TILE), BF16),
    jax.ShapeDtypeStruct((2, TILE), F32),
]


def call_prepare(*arrays):
    return pl.pallas_call(
        prepare,
        out_shape=HELD[:1] + TABLES + [jax.ShapeDtypeStruct((CHANNELS, 8, TICKS), F32)] * 2,
        in_specs=[VMEM] * len(arrays),
        out_specs=[VMEM] * 7,
        name="prepare",
        compiler_params=room(12),
    )(*arrays)


def call_cut(*arrays):
    strip = jax.ShapeDtypeStruct((CHANNELS, 24, TICKS), F32)
    return pl.pallas_call(
        cut,
        out_shape=[strip, strip] + FRONT + TABLES,
        in_specs=[pl.BlockSpec(memory_space=pl.ANY)] * 4 + [VMEM] * (len(arrays) - 4),
        out_specs=[VMEM] * 10,
        scratch_shapes=[
            pltpu.VMEM((8, CHANNELS, 8, TICKS), F32),
            pltpu.SemaphoreType.DMA((8,)),
        ],
        input_output_aliases={6 + k: 2 + k for k in range(8)},
        name="cut",
        compiler_params=room(24),
    )(*arrays)


def call_first(*arrays):
    return pl.pallas_call(
        first,
        out_shape=FRONT,
        in_specs=[SMEM] + [VMEM] * (len(arrays) - 1),
        out_specs=[VMEM] * 4,
        input_output_aliases={3: 0},
        name="first",
        compiler_params=room(24),
    )(*arrays)


def call_inner(*arrays):
    return pl.pallas_call(
        inner,
        out_shape=BACK,
        in_specs=[SMEM] + [VMEM] * (len(arrays) - 1),
        out_specs=[VMEM] * len(BACK),
        scratch_shapes=[pltpu.VMEM((24, DEEP, TILE), F32)],
        name="inner",
        compiler_params=room(24),
    )(*arrays)


def call_border(*arrays):
    field = jax.ShapeDtypeStruct((CHANNELS, WIRES, TICKS), F32)
    return pl.pallas_call(
        border,
        out_shape=[field, field, jax.ShapeDtypeStruct((16, TILE), F32)] + HELD,
        in_specs=[SMEM] + [VMEM] * (len(arrays) - 1),
        out_specs=[VMEM] * (3 + len(HELD)),
        scratch_shapes=[
            pltpu.VMEM((24, DEEP, TILE), F32),
            pltpu.VMEM((96, TILE), F32),
        ],
        input_output_aliases={3 + k: 3 + k for k in range(len(HELD))},
        name="border",
        compiler_params=room(24),
    )(*arrays)[:3]


def unpack(sums, front_taps, front_square, front_line, back_taps, back_square, back_line, factor):
    row = lax.broadcasted_iota(jnp.int32, (16, STEP, TILE), 1)
    wide = jnp.broadcast_to(sums[...][:, None, :], (16, STEP, TILE))
    wide = jnp.where(lanes(wide.shape) % STEP == row, wide, 0.0).reshape(16 * STEP, TILE)
    channel = lax.broadcasted_iota(jnp.int32, (TILE, CHANNELS), 0) // STEP
    pick = jnp.where(channel == lanes((TILE, CHANNELS)), 1.0, 0.0)
    rows = exact(wide, pick, ((1,), (0,))) * factor
    for taps, square, line, first, square_at, line_at in (
        (front_taps, front_square, front_line, 32, 80, 59),
        (back_taps, back_square, back_line, 0, 64, 27),
    ):
        for i in range(3):
            for j in range(9):
                at = first + 9 * i + j
                taps[j, i : i + 1, :] = rows[at : at + 1, :]
        square[...] = rows[square_at : square_at + CHANNELS, :]
        line[...] = rows[line_at : line_at + 1, :]


def call_unpack(sums, factor):
    shapes = [(9, 3, CHANNELS), (CHANNELS, CHANNELS), (1, CHANNELS)] * 2
    return pl.pallas_call(
        functools.partial(unpack, factor=factor),
        out_shape=[jax.ShapeDtypeStruct(shape, F32) for shape in shapes],
        in_specs=[VMEM],
        out_specs=[VMEM] * 6,
        name="unpack",
        compiler_params=room(6),
    )(sums)


def shift(value, axes, step):
    count = lax.axis_size(axes)
    pairs = [(i, i + step) for i in range(count) if 0 <= i + step < count]
    return lax.ppermute(value, axes, pairs)


def per_device(
    signal,
    kernel_front,
    mixing_front,
    offset_front,
    kernel_back,
    mixing_back,
    offset_back,
    upstream,
):
    pack = lambda part: jnp.concatenate([part[:, :PACK], part[:, PACK:]], axis=2)
    place = jnp.stack([lax.axis_index(TICK), lax.axis_index(WIRE)]).astype(jnp.int32)
    s_low, s_high = shift(signal, TICK, 1), shift(signal, TICK, -1)
    u_low = shift(pack(upstream[:, :, 64:]), TICK, 1)
    u_high = shift(pack(upstream[:, :, :64]), TICK, -1)
    sig, *tables, own_up, own_down = call_prepare(
        signal,
        upstream,
        kernel_front.reshape(CHANNELS, 27),
        kernel_back.reshape(CHANNELS, 27),
        jnp.stack([mixing_front.T, mixing_back.T, mixing_back, mixing_front]),
        jnp.stack([offset_front, offset_back]),
    )
    ahead = call_first(place, s_low, s_high, sig, *tables)
    strip_up, strip_down, *rest = call_cut(
        s_low, s_high, u_low, u_high, own_up, own_down, *ahead, *tables
    )
    ahead, tables = rest[:4], rest[4:]
    h_up, h_down = shift(strip_down, WIRE, 1), shift(strip_up, WIRE, -1)
    behind = call_inner(place, u_low, u_high, upstream, *ahead[2:], *tables)
    held = {**dict(zip(AHEAD, ahead)), **dict(zip(BEHIND, behind))}
    response, signal_grad, sums = call_border(
        place, h_up, h_down, *(held[name] for name in PLANES), *tables
    )
    for group in REDUCTION_ORDER:
        sums = lax.psum(sums, group)
    factor = 1.0 / math.sqrt(WIRES * lax.axis_size(WIRE) * TICKS * lax.axis_size(TICK))
    front_taps, front_square, front_line, back_taps, back_square, back_line = call_unpack(
        sums, factor
    )
    return (
        response,
        signal_grad,
        front_taps.transpose(2, 1, 0),
        front_square,
        front_line.reshape(CHANNELS),
        back_taps.transpose(2, 1, 0),
        back_square,
        back_line.reshape(CHANNELS),
    )


def solution(mesh):
    fine = Mesh(mesh.devices.reshape(8, 4, 2, 2, 4), TICK + WIRE)
    block = P(None, WIRE, TICK)
    in_specs = (block, P(), P(), P(), P(), P(), P(), block)
    out_specs = (block, block, P(), P(), P(), P(), P(), P())
    return jax.shard_map(
        per_device, mesh=fine, in_specs=in_specs, out_specs=out_specs, check_vma=False
    )
```
